512 devices in a mesh: replica: 64 (over x_lo, z, core), tensor: 8 (over x_hi, y).
Axes of the slice: x: 4 (x_hi: 2, x_lo: 2; x = x_hi * 2 + x_lo), y: 4, z: 16, core: 2. Of those that a mesh axis runs over, the one named last changes fastest.
Arguments:
- qkv_weight: bfloat16 [5120, 7168], P(('replica', 'tensor')), may hold values from -0.078125 to 0.078125
- qkv_bias: bfloat16 [7168], P('tensor'), may hold values from -7 to 7
- norm_gain: bfloat16 [5120], replicated, may hold values from 0.099609375 to 1.8984375
- decode_hidden: bfloat16 [1024, 5120], P('replica'), may hold values from -6 to 6
- stored_keys: bfloat16 [1024, 8, 256, 128], P('replica', 'tensor'), may hold values from -72 to 72
- stored_values: bfloat16 [1024, 8, 256, 128], P('replica', 'tensor'), may hold values from -6 to 6
- stored_lengths: int32 [64, 16], P('replica'), may hold values from 1 to 256, 2048 in all within a row
- response_hidden: bfloat16 [640, 64, 5120], P('replica', None, 'tensor'), may hold values from -6 to 6
- response_lengths: int32 [64, 10], P('replica'), may hold values from 1 to 64, 560 in all within a row
- response_target: int32 [640, 1], P('replica'), may hold values from 0 to 7; in each aligned block of 10 rows (0 to 9, 10 to 19, ...) at most 2 rows name the same one
Outputs:
- step_attention: bfloat16 [1024, 5120], P('replica', 'tensor')
- learner_attention: bfloat16 [1024, 64, 5120], P(('replica', 'tensor'))
The draws below stay inside these ranges and needn't reach their ends.
Inputs may be any that keep to these rules, and one draw needn't show every extreme that they name: `response_lengths`: the 10 lengths of one group sum to 560, and one of them equals 64. `stored_lengths`: the 16 lengths of one group sum to 2048, and one of them equals 256. `response_target`: among the 10 responses of one rollout group at most 2 name the same learner device, and in some groups one device is named by exactly 2.
All inputs are finite; a program needn't handle non-finite values.
Results may differ from the reference program's by a relative error of at most 0.0065.
The reference program's roundings to bfloat16 on the way count: a program that leaves them out, or rounds other values in their place, can miss the bound.
Values may be sent and summed in bfloat16 or wider, within the bound.
A program may use at most 64 MiB of HBM per device.

```python
import math
import jax
import jax.numpy as jnp
import numpy as np
from jax import lax

MODEL_WIDTH = 5120
QUERY_HEADS = 40
KV_HEADS = 8
HEAD_DIM = 128
DONE_PER_GROUP = 10
RESPONSE_LIMIT = 64
DECODE_PER_GROUP = 16
CACHE_LIMIT = 256
QKV = 7168
CAP = 2
DECODE_TOTAL = 1024
NRESP = 640
SLOT_TOTAL = 1024
N_REPLICA = 64
N_TENSOR = 8


def draw_qkv_bias(key, part):
    drawn = 0.5 * jnp.clip(jax.random.normal(jax.random.fold_in(key, 11), (QKV,), jnp.float32), -6.0, 6.0)
    return drawn.astype(jnp.bfloat16)


def draw_stored_keys(key, part):
    base_offset = jnp.clip(jax.random.normal(key, (DECODE_TOTAL, KV_HEADS, CACHE_LIMIT, HEAD_DIM), jnp.float32), -6.0, 6.0)
    return base_offset.astype(jnp.bfloat16)


def levels(rng, shape, pieces, low, high):
    gain, own = 1.0, jax.random.fold_in(rng, 6)
    for dim, shards_of in pieces:
        heights = jnp.exp(jax.random.uniform(jax.random.fold_in(own, dim), (shards_of,), jnp.float32, low / len(pieces), high / len(pieces)))
        gain = gain * jnp.repeat(heights, shape[dim] // shards_of).reshape([-1 if axis == dim else 1 for axis in range(len(shape))])
    return gain


def profile(count, total, bound, lean):
    weights = [(1 << 20) // math.isqrt(rank ** lean) + 1 for rank in range(2, count + 1)]
    rest, counts = total - bound - (count - 1), [1] * (count - 1)
    while rest > 0:
        free = [i for i in range(count - 1) if counts[i] < bound]
        pool, remaining = sum([weights[i] for i in free]), rest
        for i in free:
            more = min(bound - counts[i], max(1, remaining * weights[i] // pool), rest)
            counts[i] = counts[i] + more
            rest = rest - more
    return np.array([bound] + counts)


def ragged(key, number_of, total, reach, slope):
    if number_of == 2:
        one = jax.random.randint(key, (), max(1, total - reach), min(reach, total - 1) + 1)
        return jnp.stack([one, total - one])
    lengths = jnp.asarray(profile(number_of, total, reach, slope), jnp.int32)
    twos = (number_of - 1) // 2
    donor, receiver = lengths[1:1 + 2 * twos:2], lengths[2:2 + 2 * twos:2]
    margin = jnp.minimum(donor - 1, reach - receiver)
    moved = jax.random.randint(jax.random.fold_in(key, 1), (twos,), 0, 1 << 20) % (margin + 1)
    lengths = lengths.at[1:1 + 2 * twos:2].set(donor - moved).at[2:2 + 2 * twos:2].set(receiver + moved)
    return lengths[jax.random.permutation(jax.random.fold_in(key, 2), number_of)]


def shared_out(own_key, own, number, rows, count, top, bound, slope):
    sequence = jax.random.permutation(own_key, count)
    heavy_load, usual = portions_of(count, rows * top, bound, slope, True), portions_of(count, rows * top, bound, slope, False)
    places = jnp.arange(count)

    def named(lengths, offset_by):
        used = int((lengths > 0).sum())
        fixed = max(1, used // 4)
        shifted = fixed + (places - fixed + offset_by * (used - fixed)) % max(1, count - fixed)
        return jnp.zeros((count,), jnp.int32).at[sequence[jnp.where(places < fixed, places, shifted)]].set(jnp.asarray(lengths, jnp.int32))

    lengths = jnp.where(number % 4 == 0, named(heavy_load, number // 4), named(usual, number - number // 4 - 1))
    mixed = jax.random.permutation(jax.random.fold_in(own, 3), count)
    source_of, sink = mixed[0:count // 2 * 2:2], mixed[1:count // 2 * 2:2]
    margin = jnp.minimum(lengths[source_of] - 1, bound - lengths[sink]) // 2
    margin = jnp.where((source_of == sequence[0]) | (sink == sequence[0]) | (lengths[sink] == 0), 0, jnp.maximum(margin, 0))
    shifted = jax.random.randint(jax.random.fold_in(own, 4), (count // 2,), 0, 1 << 20) % (margin + 1)
    lengths = lengths.at[source_of].add(-shifted).at[sink].add(shifted)
    items = jnp.searchsorted(jnp.cumsum(lengths), jnp.arange(rows * top), side="right").astype(jnp.int32)
    table = items.reshape(top, rows).T
    table = table[jax.random.permutation(jax.random.fold_in(own, 1), rows)]
    offset_by = jax.random.randint(jax.random.fold_in(own, 2), (rows, 1), 0, top)
    return jnp.take_along_axis(table, (jnp.arange(top)[None, :] + offset_by) % top, axis=1)


def portions_of(count, total, most, slope, full):
    portions = [(1 << 20) // math.isqrt(standing ** slope) + 1 for standing in range(1, count + 1)]
    largest = most if full else min(most, max(-(-total // count), total * portions[0] // sum(portions)))
    least = 1 if total - largest >= count - 1 else 0
    holding, rest = [largest] + [least] * (count - 1), total - largest - least * (count - 1)
    while rest > 0:
        candidates = [i for i in range(1, count) if holding[i] < largest] or [i for i in range(1, count) if holding[i] < most]
        pool, left = sum([portions[i] for i in candidates]), rest
        for i in candidates:
            addition = min(most - holding[i], max(1, left * portions[i] // pool), rest)
            holding[i] = holding[i] + addition
            rest = rest - addition
    return np.array(holding)


def noise(own_key, shape, scale, bound, split=(), kind=jnp.bfloat16):
    level = levels(own_key, shape, split, -0.22, 0.18) if split else 1.0
    result = jax.random.normal(own_key, shape, jnp.float32) * scale * level
    return jnp.minimum(jnp.maximum(result, -bound), bound).astype(kind)


def setup_inputs(seed: int = 0) -> dict:
    seeds = jax.random.split(jax.random.key(seed), 11)
    qkv_weight = noise(seeds[0], (MODEL_WIDTH, QKV), MODEL_WIDTH ** -0.5, 0.078125, ((0, 512),))
    qkv_bias = draw_qkv_bias(jax.random.fold_in(seeds[10], 71), 0)
    norm_gain = jnp.clip(1.0 + 0.18 * jax.random.normal(seeds[2], (MODEL_WIDTH,), jnp.float32), 0.099609375, 1.8984375).astype(jnp.bfloat16)
    decode_hidden = noise(seeds[3], (DECODE_TOTAL, MODEL_WIDTH), 1.0, 6.0, ((0, 64),))
    stored_keys = draw_stored_keys(jax.random.fold_in(seeds[10], 71), 0)
    stored_values = noise(seeds[5], (DECODE_TOTAL, KV_HEADS, CACHE_LIMIT, HEAD_DIM), 1.0, 6.0, ((0, 64), (1, 8)))
    stored_lengths = jax.vmap(lambda own: ragged(own, DECODE_PER_GROUP, DECODE_PER_GROUP * CACHE_LIMIT // 2, CACHE_LIMIT, 2))(jax.random.split(seeds[6], N_REPLICA)).reshape((N_REPLICA, DECODE_PER_GROUP)).astype(jnp.int32)
    response_hidden = noise(seeds[7], (NRESP, RESPONSE_LIMIT, MODEL_WIDTH), 1.0, 6.0, ((0, 64), (2, 8)))
    response_lengths = jax.vmap(lambda own: ragged(own, DONE_PER_GROUP, DONE_PER_GROUP * RESPONSE_LIMIT * 7 // 8, RESPONSE_LIMIT, 2))(jax.random.split(seeds[8], N_REPLICA)).reshape((N_REPLICA, DONE_PER_GROUP)).astype(jnp.int32)
    response_target_keys = jax.random.split(jax.random.fold_in(seeds[9], 1), NRESP // DONE_PER_GROUP)
    response_target_turns = jax.random.permutation(jax.random.fold_in(seeds[9], 3), NRESP // DONE_PER_GROUP)
    response_target = jax.vmap(lambda own, number: shared_out(jax.random.fold_in(seeds[9], 2), own, number, DONE_PER_GROUP, N_TENSOR, 1, CAP, 1))(response_target_keys, response_target_turns).reshape((NRESP, 1))
    return dict(qkv_weight=qkv_weight, qkv_bias=qkv_bias, norm_gain=norm_gain, decode_hidden=decode_hidden, stored_keys=stored_keys, stored_values=stored_values, stored_lengths=stored_lengths, response_hidden=response_hidden, response_lengths=response_lengths, response_target=response_target)


def normalize(rows_in, gain_vec):
    widened = rows_in.astype(jnp.float32)
    inverse = lax.rsqrt(lax.optimization_barrier(jnp.mean(widened * widened, axis=-1, keepdims=True)) + 1e-06)
    return (widened * inverse * gain_vec.astype(jnp.float32)).astype(jnp.bfloat16)

def block_attend(qkv_rows, token_lengths):
    rollout_groups = qkv_rows.shape[3] - 2
    head_size = qkv_rows.shape[4]
    number = qkv_rows.shape[0]
    length = qkv_rows.shape[1]
    query = qkv_rows[:, :, :, :rollout_groups].astype(jnp.float32)
    key_matrix = qkv_rows[:, :, :, rollout_groups].astype(jnp.float32)
    value_matrix = qkv_rows[:, :, :, rollout_groups + 1].astype(jnp.float32)
    scores = jnp.einsum('nikgh,njkh->nkgij', query, key_matrix) / math.sqrt(head_size)
    causal = jnp.arange(length)[None, :] <= jnp.arange(length)[:, None]
    masked = jnp.where(causal, scores, -jnp.inf)
    peak = lax.optimization_barrier(jnp.max(masked, axis=-1, keepdims=True))
    powers = jnp.where(causal, jnp.exp(scores - peak), 0.0)
    probs = (powers / lax.optimization_barrier(jnp.sum(powers, axis=-1, keepdims=True))).astype(jnp.bfloat16)
    mixture = jnp.einsum('nkgij,njkh->nikgh', probs.astype(jnp.float32), value_matrix)
    in_range = jnp.arange(length)[None, :] < token_lengths[:, None]
    mixture = jnp.where(in_range[:, :, None, None, None], mixture, 0.0)
    return mixture.astype(jnp.bfloat16).reshape(number, length, -1)

def attend_decoding(qkv_rows, key_cache, value_cache, token_lengths):
    rollout_groups = qkv_rows.shape[2] - 2
    head_size = qkv_rows.shape[3]
    number = qkv_rows.shape[0]
    query = qkv_rows[:, :, :rollout_groups].astype(jnp.float32)
    new_key = qkv_rows[:, :, rollout_groups].astype(jnp.float32)
    new_value = qkv_rows[:, :, rollout_groups + 1].astype(jnp.float32)
    scores = jnp.einsum('bkgh,bklh->bkgl', query, key_cache.astype(jnp.float32)) / math.sqrt(head_size)
    self_score = jnp.einsum('bkgh,bkh->bkg', query, new_key)[..., None] / math.sqrt(head_size)
    filled = (jnp.arange(key_cache.shape[2])[None, :] < token_lengths[:, None])[:, None, None, :]
    peak = jnp.maximum(lax.optimization_barrier(jnp.max(jnp.where(filled, scores, -jnp.inf), axis=-1, keepdims=True)), self_score)
    powers = jnp.where(filled, jnp.exp(scores - peak), 0.0)
    self_power = jnp.exp(self_score - peak)
    total = lax.optimization_barrier(jnp.sum(powers, axis=-1, keepdims=True)) + self_power
    probs = (powers / total).astype(jnp.bfloat16)
    self_prob = (self_power / total).astype(jnp.bfloat16)
    mixture = jnp.einsum('bkgl,bklh->bkgh', probs.astype(jnp.float32), value_cache.astype(jnp.float32))
    mixture = mixture + self_prob.astype(jnp.float32) * new_value[:, :, None, :]
    return mixture.astype(jnp.bfloat16).reshape(number, -1)

def selector(targets, shards, slot_capacity):
    number = targets.shape[0]
    same_dest = targets[:, None] == targets[None, :]
    earlier = jnp.arange(number)[None, :] < jnp.arange(number)[:, None]
    slot_index = lax.optimization_barrier(jnp.sum((same_dest & earlier).astype(jnp.int32), axis=1))
    target_slot = targets * slot_capacity + slot_index
    return (jnp.arange(shards * slot_capacity)[:, None] == target_slot[None, :]).astype(jnp.int32)

def reference(qkv_weight, qkv_bias, norm_gain, decode_hidden, stored_keys, stored_values, stored_lengths, response_hidden, response_lengths, response_target):
    rollout_groups = QUERY_HEADS // KV_HEADS
    slot_capacity = DONE_PER_GROUP // N_TENSOR + 1
    offset = qkv_bias.astype(jnp.float32)

    def one_group(group_share):
        step_rows, key_matrix, value_matrix, decode_lengths, resp_rows, token_lengths, targets = group_share
        decode_projected = (jnp.dot(normalize(step_rows, norm_gain), qkv_weight, preferred_element_type=jnp.float32) + offset).astype(jnp.bfloat16)
        decode_output = attend_decoding(decode_projected.reshape(DECODE_PER_GROUP, KV_HEADS, rollout_groups + 2, HEAD_DIM), key_matrix, value_matrix, decode_lengths)
        flattened = normalize(resp_rows, norm_gain).reshape(DONE_PER_GROUP * RESPONSE_LIMIT, MODEL_WIDTH)
        response_projected = (jnp.dot(flattened, qkv_weight, preferred_element_type=jnp.float32) + offset).astype(jnp.bfloat16)
        attention_output = block_attend(response_projected.reshape(DONE_PER_GROUP, RESPONSE_LIMIT, KV_HEADS, rollout_groups + 2, HEAD_DIM), token_lengths)
        chooser = selector(targets, N_TENSOR, slot_capacity)
        slot_matrix = jnp.einsum('sj,jrw->srw', chooser.astype(jnp.float32), attention_output.astype(jnp.float32)).astype(jnp.bfloat16)
        return (decode_output, slot_matrix)
    group_share = (decode_hidden.reshape(N_REPLICA, DECODE_PER_GROUP, MODEL_WIDTH), stored_keys.reshape(N_REPLICA, DECODE_PER_GROUP, KV_HEADS, CACHE_LIMIT, HEAD_DIM), stored_values.reshape(N_REPLICA, DECODE_PER_GROUP, KV_HEADS, CACHE_LIMIT, HEAD_DIM), stored_lengths, response_hidden.reshape(N_REPLICA, DONE_PER_GROUP, RESPONSE_LIMIT, MODEL_WIDTH), response_lengths, response_target.reshape(N_REPLICA, DONE_PER_GROUP))
    decode_output, slot_matrix = lax.map(one_group, group_share)
    return (decode_output.reshape(DECODE_TOTAL, QUERY_HEADS * HEAD_DIM), slot_matrix.reshape(SLOT_TOTAL, RESPONSE_LIMIT, QUERY_HEADS * HEAD_DIM))
```

```python
import math

import jax
import jax.numpy as jnp
from jax import lax
from jax.experimental import pallas as pl
from jax.experimental.pallas import tpu as pltpu
from jax.sharding import PartitionSpec as P

MODEL_WIDTH = 5120
HEADS = 5
HEAD_DIM = 128
DONE = 10
LIMIT = 64
LIVE = 560
STEPS = 16
CACHE = 256
COLS = 896
FEAT = 640
OUT = 640
ROWS = LIVE + STEPS
T = 8
Z = 16
CAP = 2
CHUNKS = ((0, 144), (144, 144), (288, 144), (432, 128))
MESH = pl.DeviceIdType.MESH
F32 = jnp.float32
BF16 = jnp.bfloat16
NT = (((1,), (1,)), ((), ()))


def kernel(
    lens_ref, target_ref, stored_ref, w_ref, bias_ref, gain_ref, dec_ref, resp_ref, keys_ref, values_ref,
    dec_out, learn_out,
    piece, wbuf, xbuf, squares, inverse, acc, projected, attn, kbuf, vbuf, qdec, odec, starts, counts,
    piece_send, piece_recv, sq_send, sq_recv, x_send, x_recv, z_send, z_recv, c_send, c_recv, a_send, a_recv, local_sem,
):
    r, t = lax.axis_index("replica"), lax.axis_index("tensor")
    xl, z, core = r // 32, (r // 2) % Z, r % 2
    a, b = t // 4, t % 4

    def at(xl_, z_, core_, t_):
        return (xl_ * 32 + z_ * 2 + core_, t_)

    def tensor_peer(d):
        return (r, (t + d) % T)

    up, down = at(xl, (z + 1) % Z, core, t), at(xl, (z + Z - 1) % Z, core, t)
    mate = at(xl, z, 1 - core, t)
    y_next, y_prev = (r, a * 4 + (b + 1) % 4), (r, a * 4 + (b + 3) % 4)
    other = (1 - a) * 4
    x_mate = (r, other + b)
    sent = []

    def remote(src, dst, send, recv, device):
        copy = pltpu.make_async_remote_copy(src, dst, send, recv, device_id=device, device_id_type=MESH)
        copy.start()
        sent.append(copy)

    def arrived(dst, recv, send):
        pltpu.make_async_remote_copy(dst, dst, send, recv, device_id=mate, device_id_type=MESH).wait_recv()

    barrier = pltpu.get_barrier_semaphore()
    peers = [tensor_peer(d) for d in range(1, T)]
    peers += [at(1 - xl, z, core, (t + d) % T) for d in range(T)]
    peers += [up, down, mate]
    for peer in peers:
        pl.semaphore_signal(barrier, inc=1, device_id=peer, device_id_type=MESH)

    local = []

    def bring(src, dst):
        copy = pltpu.make_async_copy(src, dst, local_sem.at[len(local)])
        copy.start()
        local.append(copy)

    for f in range(T):
        bring(dec_ref.at[:, f * FEAT : (f + 1) * FEAT], xbuf.at[f, LIVE:ROWS, :])
    bring(w_ref.at[:, pl.ds(pl.multiple_of(t * COLS, 128), COLS)], piece.at[xl * T + t])
    bring(keys_ref, kbuf)
    bring(values_ref, vbuf)

    pl.semaphore_wait(barrier, len(peers))

    for dx in range(2):
        for d in range(T):
            if dx == 0 and d == 0:
                continue
            k = (t + d) % T
            remote(
                w_ref.at[:, pl.ds(pl.multiple_of(k * COLS, 128), COLS)],
                piece.at[xl * T + t],
                piece_send.at[dx, d],
                piece_recv.at[dx, d],
                at((xl + dx) % 2, z, core, k),
            )

    ends, total = [], jnp.int32(0)
    for j in range(DONE):
        total = total + lens_ref[0, j]
        ends.append(total)
    row = lax.broadcasted_iota(jnp.int32, (LIVE, 128), 0)
    source = row
    for j in range(DONE - 1):
        source = source + jnp.where(row >= ends[j], LIMIT - lens_ref[0, j], 0)
    lane = lax.broadcasted_iota(jnp.int32, (LIVE, 128), 1)
    chosen = jnp.concatenate(
        [jnp.where(lane + 128 * i == source, 1.0, 0.0).astype(BF16) for i in range(5)], axis=1
    )
    packed = jnp.dot(chosen, resp_ref[...], preferred_element_type=F32)
    xbuf[t, 0:LIVE, :] = packed.astype(BF16)

    def x_part(f, c):
        return xbuf.at[f, pl.ds(*CHUNKS[c]), :]

    def x_to(kind, f, c, device):
        remote(x_part(f, c), x_part(f, c), x_send.at[kind, c], x_recv.at[kind, c], device)

    def x_from(kind, f, c):
        arrived(x_part(f, c), x_recv.at[kind, c], x_send.at[kind, c])

    for c in range(4):
        x_to(0, t, c, y_next)
        x_to(1, t, c, y_prev)
        x_to(2, t, c, x_mate)

    sq = jnp.concatenate([packed * packed, jnp.zeros((640 - LIVE, FEAT), F32)], axis=0)
    wide = lax.dot_general(
        jnp.ones((8, FEAT), F32), sq, NT, precision=lax.Precision.HIGHEST, preferred_element_type=F32
    )
    sub = lax.broadcasted_iota(jnp.int32, (8, 128), 0)
    dense = jnp.zeros((8, 128), F32)
    for i in range(5):
        dense = jnp.where(sub == i, wide[:, 128 * i : 128 * (i + 1)], dense)
    squares[t] = dense
    for d in range(1, T):
        remote(squares.at[t], squares.at[t], sq_send.at[d], sq_recv.at[d], tensor_peer(d))

    def w_rows(z_, xl_, core_):
        return wbuf.at[pl.ds(pl.multiple_of(xl_ * 2560 + z_ * 160 + core_ * 80, 16), 80), :]

    local[T].wait()
    for dx in range(2):
        for d in range(T):
            if dx or d:
                slot = ((xl + dx) % 2) * T + (t + T - d) % T
                arrived(piece.at[slot], piece_recv.at[dx, d], piece_send.at[dx, d])
    for x_ in range(2):
        block = jnp.concatenate([piece[x_ * T + f].astype(F32) for f in range(T)], axis=0)
        w_rows(z, x_, core)[...] = block.astype(BF16)

    def z_hop(s):
        for x_ in range(2):
            if s < 7 or x_ == 0:
                src = w_rows((z + Z - s) % Z, x_, core)
                remote(src, src, z_send.at[0, s, x_], z_recv.at[0, s, x_], up)
            if s < 7 or x_ == 1:
                src = w_rows((z + s) % Z, x_, core)
                remote(src, src, z_send.at[1, s, x_], z_recv.at[1, s, x_], down)

    def z_step(s):
        for x_ in range(2):
            for way in range(2):
                if s == 8 and x_ != way:
                    continue
                dst = w_rows((z + (s if way else Z - s)) % Z, x_, core)
                arrived(dst, z_recv.at[way, s - 1, x_], z_send.at[way, s - 1, x_])
                if s < 7 or (s == 7 and x_ == way):
                    remote(dst, dst, z_send.at[way, s, x_], z_recv.at[way, s, x_], down if way else up)
                remote(dst, dst, c_send.at[way, s, x_], c_recv.at[way, s, x_], mate)

    def from_mate(s):
        for x_ in range(2):
            for way in range(2):
                if (s == 8 and x_ != way) or (s == 0 and way):
                    continue
                dst = w_rows((z + (s if way else Z - s)) % Z, x_, 1 - core)
                arrived(dst, c_recv.at[way, s, x_], c_send.at[way, s, x_])

    z_hop(0)
    for x_ in range(2):
        src = w_rows(z, x_, core)
        remote(src, src, c_send.at[0, 0, x_], c_recv.at[0, 0, x_], mate)

    for copy in local[:T]:
        copy.wait()
    step_sum = jnp.zeros((STEPS, 1), F32)
    for f in range(T):
        part = xbuf[f, LIVE:ROWS, :].astype(F32)
        step_sum = step_sum + jnp.sum(part * part, axis=1, keepdims=True)
    for d in range(1, T):
        slot = squares.at[(t + T - d) % T]
        arrived(slot, sq_recv.at[d], sq_send.at[d])
    total_sq = squares[0]
    for f in range(1, T):
        total_sq = total_sq + squares[f]
    inv = lax.rsqrt(total_sq * (1.0 / MODEL_WIDTH) + 1e-6)
    for i in range(5):
        inverse[128 * i : 128 * (i + 1), :] = jnp.transpose(jnp.broadcast_to(inv[i : i + 1, :], (128, 128)))
    inverse[LIVE:ROWS, :] = jnp.broadcast_to(lax.rsqrt(step_sum * (1.0 / MODEL_WIDTH) + 1e-6), (STEPS, 128))

    def multiply(f, first=False):
        parts = []
        for i in range(5):
            lanes = slice(128 * i, 128 * (i + 1))
            part = xbuf[f, :, lanes].astype(F32) * inverse[0:ROWS, :]
            parts.append((part * gain_ref[f, :, lanes]).astype(BF16))
        product = jnp.dot(
            jnp.concatenate(parts, axis=1),
            wbuf[pl.ds(pl.multiple_of(f * FEAT, 128), FEAT), :],
            preferred_element_type=F32,
        )
        acc[...] = product if first else acc[...] + product

    projected[ROWS:640, :] = jnp.zeros((640 - ROWS, COLS), BF16)
    slots, begin = [], jnp.int32(0)
    for j in range(DONE):
        earlier = jnp.int32(0)
        for i in range(j):
            earlier = earlier + jnp.where(target_ref[i, 0] == target_ref[j, 0], 1, 0)
        slots.append(target_ref[j, 0] * CAP + earlier)
    for s in range(T * CAP):
        first_row, held = jnp.int32(0), jnp.int32(0)
        for j in range(DONE):
            hit = slots[j] == s
            first_row = first_row + jnp.where(hit, ends[j] - lens_ref[0, j], 0)
            held = held + jnp.where(hit, lens_ref[0, j], 0)
        starts[s] = first_row
        counts[s] = held

    def f_next(side, d=1):
        return side + (b + d) % 4

    own = a * 4

    def own_direct(c):
        x_from(0, f_next(own, 3), c)
        if c < 2:
            x_to(3, f_next(own, 3), c, y_next)
        x_from(1, f_next(own, 1), c)
        if c >= 2:
            x_to(4, f_next(own, 1), c, y_prev)

    def mate_direct(c):
        x_from(2, other + b, c)
        x_to(5, other + b, c, y_next)
        x_to(6, other + b, c, y_prev)

    def mate_relayed(c):
        x_from(5, f_next(other, 3), c)
        if c < 2:
            x_to(7, f_next(other, 3), c, y_next)
        x_from(6, f_next(other, 1), c)
        if c >= 2:
            x_to(8, f_next(other, 1), c, y_prev)

    def far(kind, side):
        for c in range(4):
            x_from(kind if c < 2 else kind + 1, f_next(side, 2), c)

    q, p = z // 4, z % 4
    near = (q + 3 + 2 * (p // 2)) % 4
    opposite = (q + 2) % 4
    wide_side = (q + 1 + 2 * (p // 2)) % 4

    own_direct(0)
    z_step(1)
    own_direct(1)
    mate_direct(0)
    own_direct(2)
    own_direct(3)
    z_step(2)
    mate_direct(1)
    z_step(3)
    mate_direct(2)
    far(3, own)
    for s in range(4):
        from_mate(s)
    multiply(own + q, first=True)
    mate_direct(3)
    z_step(4)
    mate_relayed(0)
    mate_relayed(1)
    z_step(5)
    mate_relayed(2)
    from_mate(4)
    from_mate(5)
    multiply(own + near)
    mate_relayed(3)
    z_step(6)
    z_step(7)
    from_mate(6)
    from_mate(7)
    multiply(own + wide_side)
    far(7, other)
    multiply(other + q)
    multiply(other + near)
    z_step(8)
    multiply(other + wide_side)
    from_mate(8)
    multiply(own + opposite)
    multiply(other + opposite)

    scale = 1.0 / math.sqrt(HEAD_DIM)
    projected[0:ROWS, :] = (acc[...] + bias_ref[...]).astype(BF16)
    at_row = lax.broadcasted_iota(jnp.int32, (128, 128), 0)
    at_col = lax.broadcasted_iota(jnp.int32, (128, 128), 1)
    causal = (at_col <= at_row) & (at_col // LIMIT == at_row // LIMIT)

    def pair(d):
        k = (t + d) % T
        first_row = jnp.where(at_row < LIMIT, starts[CAP * k], starts[CAP * k + 1] - LIMIT)
        wanted = first_row + at_row
        chosen = jnp.concatenate(
            [jnp.where(at_col + 128 * i == wanted, 1.0, 0.0).astype(BF16) for i in range(5)], axis=1
        )
        rows = jnp.dot(chosen, projected[...], preferred_element_type=F32).astype(BF16)
        keys = rows[:, HEADS * HEAD_DIM : (HEADS + 1) * HEAD_DIM]
        vals = rows[:, (HEADS + 1) * HEAD_DIM :]
        held = jnp.where(at_row < LIMIT, counts[2 * k], counts[2 * k + 1] + LIMIT)
        live = at_row < held
        for g in range(HEADS):
            cols = slice(g * HEAD_DIM, (g + 1) * HEAD_DIM)
            scores = lax.dot_general(rows[:, cols], keys, NT, preferred_element_type=F32) * scale
            peak = jnp.max(jnp.where(causal, scores, -jnp.inf), axis=-1, keepdims=True)
            powers = jnp.where(causal, jnp.exp(scores - peak), 0.0)
            probs = (powers / jnp.sum(powers, axis=-1, keepdims=True)).astype(BF16)
            mixed = jnp.dot(probs, vals, preferred_element_type=F32)
            mixed = jnp.where(live, mixed, 0.0).astype(BF16)
            for h in range(CAP):
                attn[CAP * k + h, :, cols] = mixed[h * LIMIT : (h + 1) * LIMIT]

    def outgoing(k):
        return attn.at[pl.ds(CAP * k, CAP), :, :]

    def landing(f):
        return learn_out.at[:, :, pl.ds(pl.multiple_of(f * OUT, 128), OUT)]

    order = (6, 2, 5, 3, 7, 1, 4)
    for d in order:
        pair(d)
        remote(outgoing((t + d) % T), landing(t), a_send.at[d], a_recv.at[d], tensor_peer(d))
    pair(0)
    bring(outgoing(t), landing(t))

    step_rows = projected[LIVE:ROWS, :]
    k_new = step_rows[:, HEADS * HEAD_DIM : (HEADS + 1) * HEAD_DIM].astype(F32)
    v_new = step_rows[:, (HEADS + 1) * HEAD_DIM :].astype(F32)
    qdec[...] = jnp.zeros_like(qdec)
    for g in range(HEADS):
        query = step_rows[:, g * HEAD_DIM : (g + 1) * HEAD_DIM].astype(F32)
        qdec[:, g, :] = query
    odec[:, 0, :] = k_new
    odec[:, 1, :] = v_new
    local[T + 1].wait()
    local[T + 2].wait()
    seen = lax.broadcasted_iota(jnp.int32, (8, CACHE), 1)

    def request(i, carry):
        query = qdec[i]
        fresh = odec[i]
        own_score = jnp.sum(query * fresh[0:1, :], axis=-1, keepdims=True) * scale
        scores = lax.dot_general(query.astype(BF16), kbuf[i], NT, preferred_element_type=F32) * scale
        filled = seen < stored_ref[0, i]
        peak = jnp.maximum(jnp.max(jnp.where(filled, scores, -jnp.inf), axis=-1, keepdims=True), own_score)
        powers = jnp.where(filled, jnp.exp(scores - peak), 0.0)
        own_power = jnp.exp(own_score - peak)
        whole = jnp.sum(powers, axis=-1, keepdims=True) + own_power
        probs = (powers / whole).astype(BF16)
        own_prob = (own_power / whole).astype(BF16).astype(F32)
        mixed = jnp.dot(probs, vbuf[i], preferred_element_type=F32)
        odec[i] = mixed + own_prob * fresh[1:2, :]
        return carry

    lax.fori_loop(0, STEPS, request, 0)
    for g in range(HEADS):
        dec_out[:, g * HEAD_DIM : (g + 1) * HEAD_DIM] = odec[:, g, :].astype(BF16)

    local[-1].wait()
    for d in range(1, T):
        arrived(landing((t + T - d) % T), a_recv.at[d], a_send.at[d])
    for copy in sent:
        copy.wait_send()


def body(
    qkv_weight,
    qkv_bias,
    norm_gain,
    decode_hidden,
    stored_keys,
    stored_values,
    stored_lengths,
    response_hidden,
    response_lengths,
    response_target,
):
    vmem = pl.BlockSpec(memory_space=pltpu.VMEM)
    smem = pl.BlockSpec(memory_space=pltpu.SMEM)
    anywhere = pl.BlockSpec(memory_space=pl.ANY)
    dma = pltpu.SemaphoreType.DMA
    return pl.pallas_call(
        kernel,
        out_shape=(
            jax.ShapeDtypeStruct((STEPS, OUT), BF16),
            jax.ShapeDtypeStruct((CAP, LIMIT, T * OUT), BF16),
        ),
        in_specs=[smem, smem, smem, vmem, vmem, vmem, anywhere, vmem, anywhere, anywhere],
        out_specs=(vmem, anywhere),
        scratch_shapes=[
            pltpu.VMEM((2 * T, 10, COLS), BF16),
            pltpu.VMEM((MODEL_WIDTH, COLS), BF16),
            pltpu.VMEM((T, ROWS, FEAT), BF16),
            pltpu.VMEM((T, 8, 128), F32),
            pltpu.VMEM((640, 128), F32),
            pltpu.VMEM((ROWS, COLS), F32),
            pltpu.VMEM((640, COLS), BF16),
            pltpu.VMEM((T * CAP, LIMIT, OUT), BF16),
            pltpu.VMEM((STEPS, CACHE, HEAD_DIM), BF16),
            pltpu.VMEM((STEPS, CACHE, HEAD_DIM), BF16),
            pltpu.VMEM((STEPS, 8, HEAD_DIM), F32),
            pltpu.VMEM((STEPS, 8, HEAD_DIM), F32),
            pltpu.SMEM((T * CAP,), jnp.int32),
            pltpu.SMEM((T * CAP,), jnp.int32),
            dma((2, T)), dma((2, T)),
            dma((T,)), dma((T,)),
            dma((9, 4)), dma((9, 4)),
            dma((2, 8, 2)), dma((2, 8, 2)),
            dma((2, 9, 2)), dma((2, 9, 2)),
            dma((T,)), dma((T,)),
            dma((T + 4,)),
        ],
        compiler_params=pltpu.CompilerParams(
            collective_id=0, has_side_effects=True, vmem_limit_bytes=56 << 20
        ),
        name="project_and_attend",
    )(
        response_lengths,
        response_target,
        stored_lengths,
        qkv_weight,
        qkv_bias.astype(F32).reshape(1, COLS),
        norm_gain.astype(F32).reshape(T, 1, FEAT),
        decode_hidden,
        response_hidden.reshape(DONE * LIMIT, FEAT),
        stored_keys.reshape(STEPS, CACHE, HEAD_DIM),
        stored_values.reshape(STEPS, CACHE, HEAD_DIM),
    )


def solution(mesh):
    return jax.shard_map(
        body,
        mesh=mesh,
        in_specs=(
            P(("replica", "tensor"), None),
            P("tensor"),
            P(),
            P("replica", None),
            P("replica", "tensor", None, None),
            P("replica", "tensor", None, None),
            P("replica", None),
            P("replica", None, "tensor"),
            P("replica", None),
            P("replica", None),
        ),
        out_specs=(P("replica", "tensor"), P(("replica", "tensor"), None, None)),
        check_vma=False,
    )
```

```python
import math

import jax
import jax.numpy as jnp
from jax import lax
from jax.experimental import pallas as pl
from jax.experimental.pallas import tpu as pltpu
from jax.sharding import PartitionSpec as P

MODEL_WIDTH = 5120
HEADS = 5
HEAD_DIM = 128
DONE = 10
LIMIT = 64
LIVE = 560
STEPS = 16
CACHE = 256
COLS = 896
FEAT = 640
OUT = 640
ROWS = LIVE + STEPS
T = 8
Z = 16
CAP = 2
KEEP = 48
GROUP = 2
CHUNKS = ((0, 144), (144, 144), (288, 144), (432, 128))
MESH = pl.DeviceIdType.MESH
F32 = jnp.float32
BF16 = jnp.bfloat16
NT = (((1,), (1,)), ((), ()))


def kernel(
    lens_ref, target_ref, stored_ref, w_ref, bias_ref, gain_ref, dec_ref, resp_ref, keys_ref, values_ref,
    dec_out, learn_out,
    piece, wbuf, xbuf, squares, inverse, gains, acc, projected, attn, kbuf, vbuf, qdec, odec, starts, counts,
    piece_send, piece_recv, sq_send, sq_recv, x_send, x_recv, z_send, z_recv, c_send, c_recv, g_send, g_recv, a_send, a_recv, local_sem,
):
    r, t = lax.axis_index("replica"), lax.axis_index("tensor")
    xl, z, core = r // 32, (r // 2) % Z, r % 2
    a, b = t // 4, t % 4

    def at(xl_, z_, core_, t_):
        return (xl_ * 32 + z_ * 2 + core_, t_)

    def tensor_peer(d):
        return (r, (t + d) % T)

    up, down = at(xl, (z + 1) % Z, core, t), at(xl, (z + Z - 1) % Z, core, t)
    mate = at(xl, z, 1 - core, t)
    y_next, y_prev = (r, a * 4 + (b + 1) % 4), (r, a * 4 + (b + 3) % 4)
    other = (1 - a) * 4
    x_mate = (r, other + b)
    across = at(1 - xl, z, core, t)
    sent = []

    def remote(src, dst, send, recv, device):
        copy = pltpu.make_async_remote_copy(src, dst, send, recv, device_id=device, device_id_type=MESH)
        copy.start()
        sent.append(copy)

    def arrived(dst, recv, send):
        pltpu.make_async_remote_copy(dst, dst, send, recv, device_id=mate, device_id_type=MESH).wait_recv()

    barrier = pltpu.get_barrier_semaphore()
    peers = [tensor_peer(d) for d in range(1, T)]
    peers += [at(1 - xl, z, core, (t + d) % T) for d in range(T)]
    peers += [up, down, mate]
    for peer in peers:
        pl.semaphore_signal(barrier, inc=1, device_id=peer, device_id_type=MESH)

    local = []

    def bring(src, dst):
        copy = pltpu.make_async_copy(src, dst, local_sem.at[len(local)])
        copy.start()
        local.append(copy)

    for f in range(T):
        bring(dec_ref.at[:, f * FEAT : (f + 1) * FEAT], xbuf.at[f, LIVE:ROWS, :])
    bring(w_ref.at[:, pl.ds(pl.multiple_of(t * COLS, 128), COLS)], piece.at[xl * T + t])
    bring(keys_ref, kbuf)
    bring(values_ref, vbuf)

    pl.semaphore_wait(barrier, len(peers))

    for dx in range(2):
        for d in range(T):
            if dx == 0 and d == 0:
                continue
            k = (t + d) % T
            remote(
                w_ref.at[:, pl.ds(pl.multiple_of(k * COLS, 128), COLS)],
                piece.at[xl * T + t],
                piece_send.at[dx, d],
                piece_recv.at[dx, d],
                at((xl + dx) % 2, z, core, k),
            )

    ends, total = [], jnp.int32(0)
    for j in range(DONE):
        total = total + lens_ref[0, j]
        ends.append(total)
    row = lax.broadcasted_iota(jnp.int32, (LIVE, 128), 0)
    source = row
    for j in range(DONE - 1):
        source = source + jnp.where(row >= ends[j], LIMIT - lens_ref[0, j], 0)
    lane = lax.broadcasted_iota(jnp.int32, (LIVE, 128), 1)
    chosen = jnp.concatenate(
        [jnp.where(lane + 128 * i == source, 1.0, 0.0).astype(BF16) for i in range(5)], axis=1
    )
    packed = jnp.dot(chosen, resp_ref[...], preferred_element_type=F32)
    xbuf[t, 0:LIVE, :] = packed.astype(BF16)

    def x_part(f, c):
        return xbuf.at[f, pl.ds(*CHUNKS[c]), :]

    def x_to(kind, f, c, device):
        remote(x_part(f, c), x_part(f, c), x_send.at[kind, c], x_recv.at[kind, c], device)

    def x_from(kind, f, c):
        arrived(x_part(f, c), x_recv.at[kind, c], x_send.at[kind, c])

    for c in range(4):
        x_to(0, t, c, y_next)
        x_to(1, t, c, y_prev)
        x_to(2, t, c, x_mate)

    spans = ((KEEP, 80 - KEEP), (0, KEEP), (0, KEEP), (KEEP, 80 - KEEP))

    def w_part(side, way, s, part, core_):
        first, count = spans[part]
        z_ = (z + (s if way else Z - s)) % Z
        return wbuf.at[pl.ds(pl.multiple_of(side * 2560 + z_ * 160 + core_ * 80 + first, 16), count), :]

    def w_rows(way, s, part, core_):
        return w_part(1 - xl if part > 1 else xl, way, s, part, core_)

    def last_way(part):
        return 1 if part == 2 else 0

    def z_hop(way, s, part):
        rows = w_rows(way, s, part, core)
        remote(rows, rows, z_send.at[way, s, part], z_recv.at[way, s, part], down if way else up)

    def to_mate(way, s, part):
        rows = w_rows(way, s, part, core)
        remote(rows, rows, c_send.at[way, s, part], c_recv.at[way, s, part], mate)

    def z_step(s):
        for part in range(3):
            for way in range(2):
                if s == 8 and last_way(part) != way:
                    continue
                rows = w_rows(way, s, part, core)
                arrived(rows, z_recv.at[way, s - 1, part], z_send.at[way, s - 1, part])
                if s < 7 or (s == 7 and last_way(part) == way):
                    z_hop(way, s, part)
                if part == 0:
                    remote(rows, rows, g_send.at[way, s], g_recv.at[way, s], across)
                to_mate(way, s, part)

    def x_step(s):
        for way in range(2):
            if s == 8 and way:
                continue
            arrived(w_rows(way, s, 3, core), g_recv.at[way, s], g_send.at[way, s])
            to_mate(way, s, 3)

    def from_mate(s):
        for part in range(4):
            for way in range(2):
                if (s == 8 and last_way(part) != way) or (s == 0 and way):
                    continue
                arrived(w_rows(way, s, part, 1 - core), c_recv.at[way, s, part], c_send.at[way, s, part])

    def start_ring():
        local[T].wait()
        for dx in range(2):
            for d in range(T):
                if dx or d:
                    slot = ((xl + dx) % 2) * T + (t + T - d) % T
                    arrived(piece.at[slot], piece_recv.at[dx, d], piece_send.at[dx, d])
        for half in range(2):
            side = 1 - xl if half else xl
            block = jnp.concatenate([piece[side * T + f].astype(F32) for f in range(T)], axis=0)
            wbuf[pl.ds(pl.multiple_of(side * 2560 + z * 160 + core * 80, 16), 80), :] = block.astype(BF16)
            for part in range(2 * half, 2 + half):
                for way in range(2):
                    z_hop(way, 0, part)
        for part in range(4):
            to_mate(0, 0, part)

    start_ring()

    sums = jnp.sum(packed * packed, axis=1, keepdims=True)
    sums = jnp.concatenate([jnp.broadcast_to(sums, (LIVE, 128)), jnp.zeros((640 - LIVE, 128), F32)], axis=0)
    dense = jnp.concatenate(
        [jnp.transpose(sums[128 * i : 128 * (i + 1)])[0:1] for i in range(5)] + [jnp.zeros((3, 128), F32)], axis=0
    )
    squares[t] = dense
    for d in range(1, T):
        remote(squares.at[t], squares.at[t], sq_send.at[d], sq_recv.at[d], tensor_peer(d))
    for f in range(T):
        gain = gain_ref[f * FEAT : (f + 1) * FEAT].astype(F32).reshape(1, FEAT)
        gains[f] = jnp.broadcast_to(gain, (8, FEAT))

    def norms():
        for copy in local[:T]:
            copy.wait()
        step_sum = jnp.zeros((STEPS, 1), F32)
        for f in range(T):
            part = xbuf[f, LIVE:ROWS, :].astype(F32)
            step_sum = step_sum + jnp.sum(part * part, axis=1, keepdims=True)
        for d in range(1, T):
            slot = squares.at[(t + T - d) % T]
            arrived(slot, sq_recv.at[d], sq_send.at[d])
        total_sq = squares[0]
        for f in range(1, T):
            total_sq = total_sq + squares[f]
        inv = lax.rsqrt(total_sq * (1.0 / MODEL_WIDTH) + 1e-6)
        for i in range(5):
            inverse[128 * i : 128 * (i + 1), :] = jnp.transpose(jnp.broadcast_to(inv[i : i + 1, :], (128, 128)))
        inverse[LIVE:ROWS, :] = jnp.broadcast_to(lax.rsqrt(step_sum * (1.0 / MODEL_WIDTH) + 1e-6), (STEPS, 128))

    def multiply(*blocks, first=False):
        parts = []
        for f in blocks:
            for i in range(5):
                lanes = slice(128 * i, 128 * (i + 1))
                part = xbuf[f, :, lanes].astype(F32) * inverse[0:ROWS, :]
                parts.append((part * gains[f, 0:1, lanes]).astype(BF16))
        weights = [wbuf[pl.ds(pl.multiple_of(f * FEAT, 128), FEAT), :] for f in blocks]
        product = jnp.dot(
            jnp.concatenate(parts, axis=1), jnp.concatenate(weights, axis=0), preferred_element_type=F32
        )
        acc[...] = product if first else acc[...] + product

    projected[ROWS:640, :] = jnp.zeros((640 - ROWS, COLS), BF16)
    slots, begin = [], jnp.int32(0)
    for j in range(DONE):
        earlier = jnp.int32(0)
        for i in range(j):
            earlier = earlier + jnp.where(target_ref[0, i] == target_ref[0, j], 1, 0)
        slots.append(target_ref[0, j] * CAP + earlier)
    for s in range(T * CAP):
        first_row, held = jnp.int32(0), jnp.int32(0)
        for j in range(DONE):
            hit = slots[j] == s
            first_row = first_row + jnp.where(hit, ends[j] - lens_ref[0, j], 0)
            held = held + jnp.where(hit, lens_ref[0, j], 0)
        starts[s] = first_row
        counts[s] = held

    def f_next(side, d=1):
        return side + (b + d) % 4

    own = a * 4

    def own_direct(c):
        x_from(0, f_next(own, 3), c)
        if c < 2:
            x_to(3, f_next(own, 3), c, y_next)
        x_from(1, f_next(own, 1), c)
        if c >= 2:
            x_to(4, f_next(own, 1), c, y_prev)

    def mate_direct(c):
        x_from(2, other + b, c)
        x_to(5, other + b, c, y_next)
        x_to(6, other + b, c, y_prev)

    def mate_relayed(c):
        x_from(5, f_next(other, 3), c)
        if c < 2:
            x_to(7, f_next(other, 3), c, y_next)
        x_from(6, f_next(other, 1), c)
        if c >= 2:
            x_to(8, f_next(other, 1), c, y_prev)

    def far(kind, side):
        for c in range(4):
            x_from(kind if c < 2 else kind + 1, f_next(side, 2), c)

    q, p = z // 4, z % 4
    near = (q + 3 + 2 * (p // 2)) % 4
    opposite = (q + 2) % 4
    wide_side = (q + 1 + 2 * (p // 2)) % 4

    own_direct(0)
    mate_direct(0)
    z_step(1)
    own_direct(1)
    mate_direct(1)
    z_step(2)
    x_step(1)
    own_direct(2)
    mate_direct(2)
    z_step(3)
    x_step(2)
    own_direct(3)
    mate_direct(3)
    z_step(4)
    x_step(3)
    norms()
    far(3, own)
    mate_relayed(0)
    for s in range(4):
        from_mate(s)
    z_step(5)
    x_step(4)
    mate_relayed(1)
    multiply(own + q, first=True)
    z_step(6)
    x_step(5)
    mate_relayed(2)
    from_mate(4)
    from_mate(5)
    multiply(own + near)
    z_step(7)
    x_step(6)
    mate_relayed(3)
    z_step(8)
    x_step(7)
    from_mate(6)
    from_mate(7)
    multiply(own + wide_side)
    x_step(8)
    far(7, other)
    multiply(other + q, other + near, other + wide_side)
    from_mate(8)
    multiply(own + opposite, other + opposite)

    scale = 1.0 / math.sqrt(HEAD_DIM)
    projected[0:ROWS, :] = (acc[...] + bias_ref[...].astype(F32).reshape(1, COLS)).astype(BF16)
    at_row = lax.broadcasted_iota(jnp.int32, (128, 128), 0)
    at_col = lax.broadcasted_iota(jnp.int32, (128, 128), 1)
    causal = (at_col <= at_row) & (at_col // LIMIT == at_row // LIMIT)

    def learner(dx, dy):
        return (a + dx) % 2 * 4 + (b + dy) % 4

    def spread(targets):
        picks = []
        for k in targets:
            first_row = jnp.where(at_row < LIMIT, starts[CAP * k], starts[CAP * k + 1] - LIMIT)
            wanted = first_row + at_row
            picks.append(
                jnp.concatenate(
                    [jnp.where(at_col + 128 * i == wanted, 1.0, 0.0).astype(BF16) for i in range(5)], axis=1
                )
            )
        picked = jnp.dot(jnp.concatenate(picks, axis=0), projected[...], preferred_element_type=F32)
        return [picked[128 * i : 128 * (i + 1)].astype(BF16) for i in range(len(targets))]

    def pair(k, rows):
        keys = rows[:, HEADS * HEAD_DIM : (HEADS + 1) * HEAD_DIM]
        vals = rows[:, (HEADS + 1) * HEAD_DIM :]
        held = jnp.where(at_row < LIMIT, counts[2 * k], counts[2 * k + 1] + LIMIT)
        live = at_row < held
        for g in range(HEADS):
            cols = slice(g * HEAD_DIM, (g + 1) * HEAD_DIM)
            scores = lax.dot_general(rows[:, cols], keys, NT, preferred_element_type=F32) * scale
            scores = jnp.where(causal, scores, -jnp.inf)
            powers = jnp.exp(scores - jnp.max(scores, axis=-1, keepdims=True))
            probs = (powers / jnp.sum(powers, axis=-1, keepdims=True)).astype(BF16)
            mixed = jnp.dot(probs, vals, preferred_element_type=F32)
            mixed = jnp.where(live, mixed, 0.0).astype(BF16)
            for h in range(CAP):
                attn[CAP * k + h, :, cols] = mixed[h * LIMIT : (h + 1) * LIMIT]

    def outgoing(k):
        return attn.at[pl.ds(CAP * k, CAP), :, :]

    def landing(f):
        return learn_out.at[:, :, pl.ds(pl.multiple_of(f * OUT, 128), OUT)]

    order = ((1, 2), (1, 0), (1, 1), (1, 3), (0, 2), (0, 1), (0, 3))
    targets = [learner(*step) for step in order] + [t]
    for n, k in enumerate(targets):
        if n % GROUP == 0:
            spreads = spread(targets[n : n + GROUP])
        pair(k, spreads[n % GROUP])
        if n < len(order):
            remote(outgoing(k), landing(t), a_send.at[n], a_recv.at[n], (r, k))
        else:
            bring(outgoing(t), landing(t))

    step_rows = projected[LIVE:ROWS, :]
    k_new = step_rows[:, HEADS * HEAD_DIM : (HEADS + 1) * HEAD_DIM].astype(F32)
    v_new = step_rows[:, (HEADS + 1) * HEAD_DIM :].astype(F32)
    qdec[...] = jnp.zeros_like(qdec)
    for g in range(HEADS):
        query = step_rows[:, g * HEAD_DIM : (g + 1) * HEAD_DIM].astype(F32)
        qdec[:, g, :] = query
    odec[:, 0, :] = k_new
    odec[:, 1, :] = v_new
    local[T + 1].wait()
    local[T + 2].wait()
    seen = lax.broadcasted_iota(jnp.int32, (8, CACHE), 1)

    def request(i, carry):
        query = qdec[i]
        fresh = odec[i]
        own_score = jnp.sum(query * fresh[0:1, :], axis=-1, keepdims=True) * scale
        scores = lax.dot_general(query.astype(BF16), kbuf[i], NT, preferred_element_type=F32) * scale
        filled = seen < stored_ref[0, i]
        peak = jnp.maximum(jnp.max(jnp.where(filled, scores, -jnp.inf), axis=-1, keepdims=True), own_score)
        powers = jnp.where(filled, jnp.exp(scores - peak), 0.0)
        own_power = jnp.exp(own_score - peak)
        whole = jnp.sum(powers, axis=-1, keepdims=True) + own_power
        probs = (powers / whole).astype(BF16)
        own_prob = (own_power / whole).astype(BF16).astype(F32)
        mixed = jnp.dot(probs, vbuf[i], preferred_element_type=F32)
        odec[i] = mixed + own_prob * fresh[1:2, :]
        return carry

    lax.fori_loop(0, STEPS, request, 0, unroll=4)
    for g in range(HEADS):
        dec_out[:, g * HEAD_DIM : (g + 1) * HEAD_DIM] = odec[:, g, :].astype(BF16)

    local[-1].wait()
    for n, (dx, dy) in enumerate(order):
        arrived(landing(learner(dx, 4 - dy)), a_recv.at[n], a_send.at[n])
    for copy in sent:
        copy.wait_send()


def hand_over(step_in, learner_in, step_out, learner_out, step_buf, buf, sem):
    def learner_part(ref, i):
        return ref.at[i // 4, (i % 4) * 16 : (i % 4 + 1) * 16, :]

    n = CAP * 4
    copies = [pltpu.make_async_copy(learner_part(learner_in, i), buf.at[i], sem.at[i]) for i in range(n)]
    copies.append(pltpu.make_async_copy(step_in, step_buf, sem.at[n]))
    outs = [pltpu.make_async_copy(buf.at[i], learner_part(learner_out, i), sem.at[n + 1 + i]) for i in range(n)]
    outs.append(pltpu.make_async_copy(step_buf, step_out, sem.at[2 * n + 1]))
    for copy in copies:
        copy.start()
    for copy, out in zip(copies, outs):
        copy.wait()
        out.start()
    for out in outs:
        out.wait()


def body(
    qkv_weight,
    qkv_bias,
    norm_gain,
    decode_hidden,
    stored_keys,
    stored_values,
    stored_lengths,
    response_hidden,
    response_lengths,
    response_target,
):
    vmem = pl.BlockSpec(memory_space=pltpu.VMEM)
    smem = pl.BlockSpec(memory_space=pltpu.SMEM)
    anywhere = pl.BlockSpec(memory_space=pl.ANY)
    dma = pltpu.SemaphoreType.DMA
    step, learner = pl.pallas_call(
        kernel,
        out_shape=(
            jax.ShapeDtypeStruct((STEPS, OUT), BF16),
            jax.ShapeDtypeStruct((CAP, LIMIT, T * OUT), BF16),
        ),
        in_specs=[smem, smem, smem, vmem, vmem, vmem, anywhere, vmem, anywhere, anywhere],
        out_specs=(vmem, anywhere),
        scratch_shapes=[
            pltpu.VMEM((2 * T, 10, COLS), BF16),
            pltpu.VMEM((MODEL_WIDTH, COLS), BF16),
            pltpu.VMEM((T, ROWS, FEAT), BF16),
            pltpu.VMEM((T, 8, 128), F32),
            pltpu.VMEM((640, 128), F32),
            pltpu.VMEM((T, 8, FEAT), F32),
            pltpu.VMEM((ROWS, COLS), F32),
            pltpu.VMEM((640, COLS), BF16),
            pltpu.VMEM((T * CAP, LIMIT, OUT), BF16),
            pltpu.VMEM((STEPS, CACHE, HEAD_DIM), BF16),
            pltpu.VMEM((STEPS, CACHE, HEAD_DIM), BF16),
            pltpu.VMEM((STEPS, 8, HEAD_DIM), F32),
            pltpu.VMEM((STEPS, 8, HEAD_DIM), F32),
            pltpu.SMEM((T * CAP,), jnp.int32),
            pltpu.SMEM((T * CAP,), jnp.int32),
            dma((2, T)), dma((2, T)),
            dma((T,)), dma((T,)),
            dma((9, 4)), dma((9, 4)),
            dma((2, 8, 3)), dma((2, 8, 3)),
            dma((2, 9, 4)), dma((2, 9, 4)),
            dma((2, 9)), dma((2, 9)),
            dma((T,)), dma((T,)),
            dma((T + 4,)),
        ],
        compiler_params=pltpu.CompilerParams(
            collective_id=0, has_side_effects=True, vmem_limit_bytes=56 << 20
        ),
        name="project_and_attend",
    )(
        response_lengths,
        response_target.reshape(1, DONE),
        stored_lengths,
        qkv_weight,
        qkv_bias,
        norm_gain,
        decode_hidden,
        response_hidden.reshape(DONE * LIMIT, FEAT),
        stored_keys.reshape(STEPS, CACHE, HEAD_DIM),
        stored_values.reshape(STEPS, CACHE, HEAD_DIM),
    )
    return pl.pallas_call(
        hand_over,
        out_shape=(
            jax.ShapeDtypeStruct(step.shape, BF16),
            jax.ShapeDtypeStruct(learner.shape, BF16),
        ),
        in_specs=[anywhere, anywhere],
        out_specs=(anywhere, anywhere),
        scratch_shapes=[
            pltpu.VMEM(step.shape, BF16),
            pltpu.VMEM((CAP * 4, 16, T * OUT), BF16),
            dma((2 + CAP * 8,)),
        ],
        name="hand_over",
    )(step, learner)


def solution(mesh):
    return jax.shard_map(
        body,
        mesh=mesh,
        in_specs=(
            P(("replica", "tensor"), None),
            P("tensor"),
            P(),
            P("replica", None),
            P("replica", "tensor", None, None),
            P("replica", "tensor", None, None),
            P("replica", None),
            P("replica", None, "tensor"),
            P("replica", None),
            P("replica", None),
        ),
        out_specs=(P("replica", "tensor"), P(("replica", "tensor"), None, None)),
        check_vma=False,
    )
```

```python
import math

import jax
import jax.numpy as jnp
from jax import lax
from jax.experimental import pallas as pl
from jax.experimental.pallas import tpu as pltpu
from jax.sharding import PartitionSpec as P

MODEL_WIDTH = 5120
HEADS = 5
HEAD_DIM = 128
DONE = 10
LIMIT = 64
LIVE = 560
STEPS = 16
CACHE = 256
COLS = 896
FEAT = 640
OUT = 640
ROWS = LIVE + STEPS
T = 8
Z = 16
CAP = 2
KEEP = 32
GROUP = 2
CHUNKS = ((0, 144), (144, 144), (288, 144), (432, 128))
MESH = pl.DeviceIdType.MESH
F32 = jnp.float32
BF16 = jnp.bfloat16
NT = (((1,), (1,)), ((), ()))


def kernel(
    lens_ref, target_ref, stored_ref, w_ref, bias_ref, gain_ref, dec_ref, resp_ref, keys_ref, values_ref,
    dec_out, learn_out,
    piece, wbuf, xbuf, squares, inverse, gains, acc, projected, attn, kbuf, vbuf, qdec, odec, starts, counts,
    piece_send, piece_recv, sq_send, sq_recv, x_send, x_recv, z_send, z_recv, c_send, c_recv, g_send, g_recv, a_send, a_recv, local_sem,
):
    r, t = lax.axis_index("replica"), lax.axis_index("tensor")
    xl, z, core = r // 32, (r // 2) % Z, r % 2
    a, b = t // 4, t % 4

    def at(xl_, z_, core_, t_):
        return (xl_ * 32 + z_ * 2 + core_, t_)

    def tensor_peer(d):
        return (r, (t + d) % T)

    up, down = at(xl, (z + 1) % Z, core, t), at(xl, (z + Z - 1) % Z, core, t)
    mate = at(xl, z, 1 - core, t)
    y_next, y_prev = (r, a * 4 + (b + 1) % 4), (r, a * 4 + (b + 3) % 4)
    other = (1 - a) * 4
    x_mate = (r, other + b)
    across = at(1 - xl, z, core, t)
    sent = []

    def remote(src, dst, send, recv, device):
        copy = pltpu.make_async_remote_copy(src, dst, send, recv, device_id=device, device_id_type=MESH)
        copy.start()
        sent.append(copy)

    def arrived(dst, recv, send):
        pltpu.make_async_remote_copy(dst, dst, send, recv, device_id=mate, device_id_type=MESH).wait_recv()

    barrier = pltpu.get_barrier_semaphore()
    peers = [tensor_peer(d) for d in range(1, T)]
    peers += [at(1 - xl, z, core, (t + d) % T) for d in range(T)]
    peers += [up, down, mate]
    for peer in peers:
        pl.semaphore_signal(barrier, inc=1, device_id=peer, device_id_type=MESH)

    local = []

    def bring(src, dst):
        copy = pltpu.make_async_copy(src, dst, local_sem.at[len(local)])
        copy.start()
        local.append(copy)

    for f in range(T):
        bring(dec_ref.at[:, f * FEAT : (f + 1) * FEAT], xbuf.at[f, LIVE:ROWS, :])
    bring(w_ref.at[:, pl.ds(pl.multiple_of(t * COLS, 128), COLS)], piece.at[xl * T + t])
    bring(keys_ref, kbuf)
    bring(values_ref, vbuf)

    pl.semaphore_wait(barrier, len(peers))

    for dx in range(2):
        for d in range(T):
            if dx == 0 and d == 0:
                continue
            k = (t + d) % T
            remote(
                w_ref.at[:, pl.ds(pl.multiple_of(k * COLS, 128), COLS)],
                piece.at[xl * T + t],
                piece_send.at[dx, d],
                piece_recv.at[dx, d],
                at((xl + dx) % 2, z, core, k),
            )

    ends, total = [], jnp.int32(0)
    for j in range(DONE):
        total = total + lens_ref[0, j]
        ends.append(total)
    row = lax.broadcasted_iota(jnp.int32, (LIVE, 128), 0)
    source = row
    for j in range(DONE - 1):
        source = source + jnp.where(row >= ends[j], LIMIT - lens_ref[0, j], 0)
    lane = lax.broadcasted_iota(jnp.int32, (LIVE, 128), 1)
    chosen = jnp.concatenate(
        [jnp.where(lane + 128 * i == source, 1.0, 0.0).astype(BF16) for i in range(5)], axis=1
    )
    packed = jnp.dot(chosen, resp_ref[...], preferred_element_type=F32)
    xbuf[t, 0:LIVE, :] = packed.astype(BF16)

    def x_part(f, c):
        return xbuf.at[f, pl.ds(*CHUNKS[c]), :]

    def x_to(kind, f, c, device):
        remote(x_part(f, c), x_part(f, c), x_send.at[kind, c], x_recv.at[kind, c], device)

    def x_from(kind, f, c):
        arrived(x_part(f, c), x_recv.at[kind, c], x_send.at[kind, c])

    for c in range(4):
        x_to(0, t, c, y_next)
        x_to(1, t, c, y_prev)
        x_to(2, t, c, x_mate)

    spans = ((KEEP, 80 - KEEP), (0, KEEP), (0, KEEP), (KEEP, 80 - KEEP))

    def w_part(side, way, s, part, core_):
        first, count = spans[part]
        z_ = (z + (s if way else Z - s)) % Z
        return wbuf.at[pl.ds(pl.multiple_of(side * 2560 + z_ * 160 + core_ * 80 + first, 16), count), :]

    def w_rows(way, s, part, core_):
        return w_part(1 - xl if part > 1 else xl, way, s, part, core_)

    def last_way(part):
        return 1 if part == 2 else 0

    def z_hop(way, s, part):
        rows = w_rows(way, s, part, core)
        remote(rows, rows, z_send.at[way, s, part], z_recv.at[way, s, part], down if way else up)

    def to_mate(way, s, part):
        rows = w_rows(way, s, part, core)
        remote(rows, rows, c_send.at[way, s, part], c_recv.at[way, s, part], mate)

    def z_step(s):
        for part in range(3):
            for way in range(2):
                if s == 8 and last_way(part) != way:
                    continue
                rows = w_rows(way, s, part, core)
                arrived(rows, z_recv.at[way, s - 1, part], z_send.at[way, s - 1, part])
                if s < 7 or (s == 7 and last_way(part) == way):
                    z_hop(way, s, part)
                if part == 0:
                    remote(rows, rows, g_send.at[way, s], g_recv.at[way, s], across)
                to_mate(way, s, part)

    def x_step(s):
        for way in range(2):
            if s == 8 and way:
                continue
            arrived(w_rows(way, s, 3, core), g_recv.at[way, s], g_send.at[way, s])
            to_mate(way, s, 3)

    def from_mate(s):
        for part in range(4):
            for way in range(2):
                if (s == 8 and last_way(part) != way) or (s == 0 and way):
                    continue
                arrived(w_rows(way, s, part, 1 - core), c_recv.at[way, s, part], c_send.at[way, s, part])

    def start_ring():
        local[T].wait()
        for dx in range(2):
            for d in range(T):
                if dx or d:
                    slot = ((xl + dx) % 2) * T + (t + T - d) % T
                    arrived(piece.at[slot], piece_recv.at[dx, d], piece_send.at[dx, d])
        for half in range(2):
            side = 1 - xl if half else xl
            block = jnp.concatenate([piece[side * T + f].astype(F32) for f in range(T)], axis=0)
            wbuf[pl.ds(pl.multiple_of(side * 2560 + z * 160 + core * 80, 16), 80), :] = block.astype(BF16)
            for part in range(2 * half, 2 + half):
                for way in range(2):
                    z_hop(way, 0, part)
        for part in range(4):
            to_mate(0, 0, part)

    start_ring()

    sums = jnp.sum(packed * packed, axis=1, keepdims=True)
    sums = jnp.concatenate([jnp.broadcast_to(sums, (LIVE, 128)), jnp.zeros((640 - LIVE, 128), F32)], axis=0)
    dense = jnp.concatenate(
        [jnp.transpose(sums[128 * i : 128 * (i + 1)])[0:1] for i in range(5)] + [jnp.zeros((3, 128), F32)], axis=0
    )
    squares[t] = dense
    for d in range(1, T):
        remote(squares.at[t], squares.at[t], sq_send.at[d], sq_recv.at[d], tensor_peer(d))
    for f in range(T):
        gain = gain_ref[f * FEAT : (f + 1) * FEAT].astype(F32).reshape(1, FEAT)
        gains[f] = jnp.broadcast_to(gain, (8, FEAT))

    def norms():
        for copy in local[:T]:
            copy.wait()
        step_sum = jnp.zeros((STEPS, 1), F32)
        for f in range(T):
            part = xbuf[f, LIVE:ROWS, :].astype(F32)
            step_sum = step_sum + jnp.sum(part * part, axis=1, keepdims=True)
        for d in range(1, T):
            slot = squares.at[(t + T - d) % T]
            arrived(slot, sq_recv.at[d], sq_send.at[d])
        total_sq = squares[0]
        for f in range(1, T):
            total_sq = total_sq + squares[f]
        inv = lax.rsqrt(total_sq * (1.0 / MODEL_WIDTH) + 1e-6)
        for i in range(5):
            inverse[128 * i : 128 * (i + 1), :] = jnp.transpose(jnp.broadcast_to(inv[i : i + 1, :], (128, 128)))
        inverse[LIVE:ROWS, :] = jnp.broadcast_to(lax.rsqrt(step_sum * (1.0 / MODEL_WIDTH) + 1e-6), (STEPS, 128))

    def multiply(*blocks, first=False):
        parts = []
        for f in blocks:
            for i in range(5):
                lanes = slice(128 * i, 128 * (i + 1))
                part = xbuf[f, :, lanes].astype(F32) * inverse[0:ROWS, :]
                parts.append((part * gains[f, 0:1, lanes]).astype(BF16))
        weights = [wbuf[pl.ds(pl.multiple_of(f * FEAT, 128), FEAT), :] for f in blocks]
        product = jnp.dot(
            jnp.concatenate(parts, axis=1), jnp.concatenate(weights, axis=0), preferred_element_type=F32
        )
        acc[...] = product if first else acc[...] + product

    projected[ROWS:640, :] = jnp.zeros((640 - ROWS, COLS), BF16)
    slots, begin = [], jnp.int32(0)
    for j in range(DONE):
        earlier = jnp.int32(0)
        for i in range(j):
            earlier = earlier + jnp.where(target_ref[0, i] == target_ref[0, j], 1, 0)
        slots.append(target_ref[0, j] * CAP + earlier)
    for s in range(T * CAP):
        first_row, held = jnp.int32(0), jnp.int32(0)
        for j in range(DONE):
            hit = slots[j] == s
            first_row = first_row + jnp.where(hit, ends[j] - lens_ref[0, j], 0)
            held = held + jnp.where(hit, lens_ref[0, j], 0)
        starts[s] = first_row
        counts[s] = held

    def f_next(side, d=1):
        return side + (b + d) % 4

    own = a * 4

    def own_direct(c):
        x_from(0, f_next(own, 3), c)
        if c < 2:
            x_to(3, f_next(own, 3), c, y_next)
        x_from(1, f_next(own, 1), c)
        if c >= 2:
            x_to(4, f_next(own, 1), c, y_prev)

    def mate_direct(c):
        x_from(2, other + b, c)
        x_to(5, other + b, c, y_next)
        x_to(6, other + b, c, y_prev)

    def mate_relayed(c):
        x_from(5, f_next(other, 3), c)
        if c < 2:
            x_to(7, f_next(other, 3), c, y_next)
        x_from(6, f_next(other, 1), c)
        if c >= 2:
            x_to(8, f_next(other, 1), c, y_prev)

    def far(kind, side):
        for c in range(4):
            x_from(kind if c < 2 else kind + 1, f_next(side, 2), c)

    q, p = z // 4, z % 4
    near = (q + 3 + 2 * (p // 2)) % 4
    opposite = (q + 2) % 4
    wide_side = (q + 1 + 2 * (p // 2)) % 4

    own_direct(0)
    mate_direct(0)
    z_step(1)
    own_direct(1)
    mate_direct(1)
    z_step(2)
    own_direct(2)
    mate_direct(2)
    x_step(1)
    z_step(3)
    own_direct(3)
    mate_direct(3)
    x_step(2)
    z_step(4)
    x_step(3)
    norms()
    z_step(5)
    mate_relayed(0)
    x_step(4)
    far(3, own)
    for s in range(4):
        from_mate(s)
    multiply(own + q, first=True)
    z_step(6)
    mate_relayed(1)
    mate_relayed(2)
    x_step(5)
    from_mate(4)
    z_step(7)
    mate_relayed(3)
    x_step(6)
    from_mate(5)
    multiply(own + near)
    z_step(8)
    x_step(7)
    from_mate(6)
    from_mate(7)
    x_step(8)
    multiply(own + wide_side)
    from_mate(8)
    multiply(own + opposite)
    far(7, other)
    multiply(other + q, other + near, other + wide_side, other + opposite)

    scale = 1.0 / math.sqrt(HEAD_DIM)
    projected[0:ROWS, :] = (acc[...] + bias_ref[...].astype(F32).reshape(1, COLS)).astype(BF16)
    at_row = lax.broadcasted_iota(jnp.int32, (128, 128), 0)
    at_col = lax.broadcasted_iota(jnp.int32, (128, 128), 1)
    causal = (at_col <= at_row) & (at_col // LIMIT == at_row // LIMIT)

    def learner(dx, dy):
        return (a + dx) % 2 * 4 + (b + dy) % 4

    def spread(targets):
        picks = []
        for k in targets:
            first_row = jnp.where(at_row < LIMIT, starts[CAP * k], starts[CAP * k + 1] - LIMIT)
            wanted = first_row + at_row
            picks.append(
                jnp.concatenate(
                    [jnp.where(at_col + 128 * i == wanted, 1.0, 0.0).astype(BF16) for i in range(5)], axis=1
                )
            )
        picked = jnp.dot(jnp.concatenate(picks, axis=0), projected[...], preferred_element_type=F32)
        return [picked[128 * i : 128 * (i + 1)].astype(BF16) for i in range(len(targets))]

    def pair(k, rows):
        keys = rows[:, HEADS * HEAD_DIM : (HEADS + 1) * HEAD_DIM]
        vals = rows[:, (HEADS + 1) * HEAD_DIM :]
        held = jnp.where(at_row < LIMIT, counts[2 * k], counts[2 * k + 1] + LIMIT)
        live = at_row < held
        for g in range(HEADS):
            cols = slice(g * HEAD_DIM, (g + 1) * HEAD_DIM)
            scores = lax.dot_general(rows[:, cols], keys, NT, preferred_element_type=F32) * scale
            scores = jnp.where(causal, scores, -jnp.inf)
            powers = jnp.exp(scores - jnp.max(scores, axis=-1, keepdims=True))
            probs = (powers / jnp.sum(powers, axis=-1, keepdims=True)).astype(BF16)
            mixed = jnp.dot(probs, vals, preferred_element_type=F32)
            mixed = jnp.where(live, mixed, 0.0).astype(BF16)
            for h in range(CAP):
                attn[CAP * k + h, :, cols] = mixed[h * LIMIT : (h + 1) * LIMIT]

    def outgoing(k):
        return attn.at[pl.ds(CAP * k, CAP), :, :]

    def landing(f):
        return learn_out.at[:, :, pl.ds(pl.multiple_of(f * OUT, 128), OUT)]

    order = ((1, 2), (0, 2), (1, 1), (0, 1), (1, 3), (1, 0), (0, 3))
    targets = [learner(*step) for step in order] + [t]
    for n, k in enumerate(targets):
        if n % GROUP == 0:
            spreads = spread(targets[n : n + GROUP])
        pair(k, spreads[n % GROUP])
        if n < len(order):
            remote(outgoing(k), landing(t), a_send.at[n], a_recv.at[n], (r, k))
        else:
            bring(outgoing(t), landing(t))

    step_rows = projected[LIVE:ROWS, :]
    k_new = step_rows[:, HEADS * HEAD_DIM : (HEADS + 1) * HEAD_DIM].astype(F32)
    v_new = step_rows[:, (HEADS + 1) * HEAD_DIM :].astype(F32)
    qdec[...] = jnp.zeros_like(qdec)
    for g in range(HEADS):
        query = step_rows[:, g * HEAD_DIM : (g + 1) * HEAD_DIM].astype(F32)
        qdec[:, g, :] = query
    odec[:, 0, :] = k_new
    odec[:, 1, :] = v_new
    local[T + 1].wait()
    local[T + 2].wait()
    seen = lax.broadcasted_iota(jnp.int32, (8, CACHE), 1)

    def request(i, carry):
        query = qdec[i]
        fresh = odec[i]
        own_score = jnp.sum(query * fresh[0:1, :], axis=-1, keepdims=True) * scale
        scores = lax.dot_general(query.astype(BF16), kbuf[i], NT, preferred_element_type=F32) * scale
        filled = seen < stored_ref[0, i]
        peak = jnp.maximum(jnp.max(jnp.where(filled, scores, -jnp.inf), axis=-1, keepdims=True), own_score)
        powers = jnp.where(filled, jnp.exp(scores - peak), 0.0)
        own_power = jnp.exp(own_score - peak)
        whole = jnp.sum(powers, axis=-1, keepdims=True) + own_power
        probs = (powers / whole).astype(BF16)
        own_prob = (own_power / whole).astype(BF16).astype(F32)
        mixed = jnp.dot(probs, vbuf[i], preferred_element_type=F32)
        odec[i] = mixed + own_prob * fresh[1:2, :]
        return carry

    lax.fori_loop(0, STEPS, request, 0, unroll=4)
    for g in range(HEADS):
        dec_out[:, g * HEAD_DIM : (g + 1) * HEAD_DIM] = odec[:, g, :].astype(BF16)

    local[-1].wait()
    for n, (dx, dy) in enumerate(order):
        arrived(landing(learner(dx, 4 - dy)), a_recv.at[n], a_send.at[n])
    for copy in sent:
        copy.wait_send()


def hand_over(step_in, learner_in, step_out, learner_out, step_buf, buf, sem):
    def learner_part(ref, i):
        return ref.at[i // 4, (i % 4) * 16 : (i % 4 + 1) * 16, :]

    n = CAP * 4
    copies = [pltpu.make_async_copy(learner_part(learner_in, i), buf.at[i], sem.at[i]) for i in range(n)]
    copies.append(pltpu.make_async_copy(step_in, step_buf, sem.at[n]))
    outs = [pltpu.make_async_copy(buf.at[i], learner_part(learner_out, i), sem.at[n + 1 + i]) for i in range(n)]
    outs.append(pltpu.make_async_copy(step_buf, step_out, sem.at[2 * n + 1]))
    for copy in copies:
        copy.start()
    for copy, out in zip(copies, outs):
        copy.wait()
        out.start()
    for out in outs:
        out.wait()


def body(
    qkv_weight,
    qkv_bias,
    norm_gain,
    decode_hidden,
    stored_keys,
    stored_values,
    stored_lengths,
    response_hidden,
    response_lengths,
    response_target,
):
    vmem = pl.BlockSpec(memory_space=pltpu.VMEM)
    smem = pl.BlockSpec(memory_space=pltpu.SMEM)
    anywhere = pl.BlockSpec(memory_space=pl.ANY)
    dma = pltpu.SemaphoreType.DMA
    step, learner = pl.pallas_call(
        kernel,
        out_shape=(
            jax.ShapeDtypeStruct((STEPS, OUT), BF16),
            jax.ShapeDtypeStruct((CAP, LIMIT, T * OUT), BF16),
        ),
        in_specs=[smem, smem, smem, vmem, vmem, vmem, anywhere, vmem, anywhere, anywhere],
        out_specs=(vmem, anywhere),
        scratch_shapes=[
            pltpu.VMEM((2 * T, 10, COLS), BF16),
            pltpu.VMEM((MODEL_WIDTH, COLS), BF16),
            pltpu.VMEM((T, ROWS, FEAT), BF16),
            pltpu.VMEM((T, 8, 128), F32),
            pltpu.VMEM((640, 128), F32),
            pltpu.VMEM((T, 8, FEAT), F32),
            pltpu.VMEM((ROWS, COLS), F32),
            pltpu.VMEM((640, COLS), BF16),
            pltpu.VMEM((T * CAP, LIMIT, OUT), BF16),
            pltpu.VMEM((STEPS, CACHE, HEAD_DIM), BF16),
            pltpu.VMEM((STEPS, CACHE, HEAD_DIM), BF16),
            pltpu.VMEM((STEPS, 8, HEAD_DIM), F32),
            pltpu.VMEM((STEPS, 8, HEAD_DIM), F32),
            pltpu.SMEM((T * CAP,), jnp.int32),
            pltpu.SMEM((T * CAP,), jnp.int32),
            dma((2, T)), dma((2, T)),
            dma((T,)), dma((T,)),
            dma((9, 4)), dma((9, 4)),
            dma((2, 8, 3)), dma((2, 8, 3)),
            dma((2, 9, 4)), dma((2, 9, 4)),
            dma((2, 9)), dma((2, 9)),
            dma((T,)), dma((T,)),
            dma((T + 4,)),
        ],
        compiler_params=pltpu.CompilerParams(
            collective_id=0, has_side_effects=True, vmem_limit_bytes=56 << 20
        ),
        name="project_and_attend",
    )(
        response_lengths,
        response_target.reshape(1, DONE),
        stored_lengths,
        qkv_weight,
        qkv_bias,
        norm_gain,
        decode_hidden,
        response_hidden.reshape(DONE * LIMIT, FEAT),
        stored_keys.reshape(STEPS, CACHE, HEAD_DIM),
        stored_values.reshape(STEPS, CACHE, HEAD_DIM),
    )
    return pl.pallas_call(
        hand_over,
        out_shape=(
            jax.ShapeDtypeStruct(step.shape, BF16),
            jax.ShapeDtypeStruct(learner.shape, BF16),
        ),
        in_specs=[anywhere, anywhere],
        out_specs=(anywhere, anywhere),
        scratch_shapes=[
            pltpu.VMEM(step.shape, BF16),
            pltpu.VMEM((CAP * 4, 16, T * OUT), BF16),
            dma((2 + CAP * 8,)),
        ],
        name="hand_over",
    )(step, learner)


def solution(mesh):
    return jax.shard_map(
        body,
        mesh=mesh,
        in_specs=(
            P(("replica", "tensor"), None),
            P("tensor"),
            P(),
            P("replica", None),
            P("replica", "tensor", None, None),
            P("replica", "tensor", None, None),
            P("replica", None),
            P("replica", None, "tensor"),
            P("replica", None),
            P("replica", None),
        ),
        out_specs=(P("replica", "tensor"), P(("replica", "tensor"), None, None)),
        check_vma=False,
    )
```

```python
import math

import jax
import jax.numpy as jnp
from jax import lax
from jax.experimental import pallas as pl
from jax.experimental.pallas import tpu as pltpu
from jax.sharding import PartitionSpec as P

MODEL_WIDTH = 5120
HEADS = 5
HEAD_DIM = 128
DONE = 10
LIMIT = 64
LIVE = 560
STEPS = 16
CACHE = 256
COLS = 896
FEAT = 640
OUT = 640
ROWS = LIVE + STEPS
T = 8
Z = 16
CAP = 2
KEEP = 32
GROUP = 2
CHUNKS = ((0, 144), (144, 144), (288, 144), (432, 128))
MESH = pl.DeviceIdType.MESH
F32 = jnp.float32
BF16 = jnp.bfloat16
NT = (((1,), (1,)), ((), ()))


def kernel(
    lens_ref, target_ref, stored_ref, w_ref, bias_ref, gain_ref, dec_ref, resp_ref, keys_ref, values_ref,
    dec_out, learn_out,
    piece, wbuf, xbuf, squares, inverse, gains, acc, projected, attn, kbuf, vbuf, qdec, odec, starts, counts,
    piece_send, piece_recv, sq_send, sq_recv, x_send, x_recv, z_send, z_recv, c_send, c_recv, g_send, g_recv, a_send, a_recv, local_sem,
):
    r, t = lax.axis_index("replica"), lax.axis_index("tensor")
    xl, z, core = r // 32, (r // 2) % Z, r % 2
    a, b = t // 4, t % 4

    def at(xl_, z_, core_, t_):
        return (xl_ * 32 + z_ * 2 + core_, t_)

    def tensor_peer(d):
        return (r, (t + d) % T)

    up, down = at(xl, (z + 1) % Z, core, t), at(xl, (z + Z - 1) % Z, core, t)
    mate = at(xl, z, 1 - core, t)
    y_next, y_prev = (r, a * 4 + (b + 1) % 4), (r, a * 4 + (b + 3) % 4)
    other = (1 - a) * 4
    x_mate = (r, other + b)
    across = at(1 - xl, z, core, t)
    sent = []

    def remote(src, dst, send, recv, device):
        copy = pltpu.make_async_remote_copy(src, dst, send, recv, device_id=device, device_id_type=MESH)
        copy.start()
        sent.append(copy)

    def arrived(dst, recv, send):
        pltpu.make_async_remote_copy(dst, dst, send, recv, device_id=mate, device_id_type=MESH).wait_recv()

    barrier = pltpu.get_barrier_semaphore()
    peers = [tensor_peer(d) for d in range(1, T)]
    peers += [at(1 - xl, z, core, (t + d) % T) for d in range(T)]
    peers += [up, down, mate]
    for peer in peers:
        pl.semaphore_signal(barrier, inc=1, device_id=peer, device_id_type=MESH)

    local = []

    def bring(src, dst):
        copy = pltpu.make_async_copy(src, dst, local_sem.at[len(local)])
        copy.start()
        local.append(copy)

    for f in range(T):
        bring(dec_ref.at[:, f * FEAT : (f + 1) * FEAT], xbuf.at[f, LIVE:ROWS, :])
    bring(w_ref.at[:, pl.ds(pl.multiple_of(t * COLS, 128), COLS)], piece.at[xl * T + t])
    bring(keys_ref, kbuf)
    bring(values_ref, vbuf)

    pl.semaphore_wait(barrier, len(peers))

    for dx in range(2):
        for d in range(T):
            if dx == 0 and d == 0:
                continue
            k = (t + d) % T
            remote(
                w_ref.at[:, pl.ds(pl.multiple_of(k * COLS, 128), COLS)],
                piece.at[xl * T + t],
                piece_send.at[dx, d],
                piece_recv.at[dx, d],
                at((xl + dx) % 2, z, core, k),
            )

    ends, total = [], jnp.int32(0)
    for j in range(DONE):
        total = total + lens_ref[0, j]
        ends.append(total)
    row = lax.broadcasted_iota(jnp.int32, (LIVE, 128), 0)
    source = row
    for j in range(DONE - 1):
        source = source + jnp.where(row >= ends[j], LIMIT - lens_ref[0, j], 0)
    lane = lax.broadcasted_iota(jnp.int32, (LIVE, 128), 1)
    chosen = jnp.concatenate(
        [jnp.where(lane + 128 * i == source, 1.0, 0.0).astype(BF16) for i in range(5)], axis=1
    )
    packed = jnp.dot(chosen, resp_ref[...], preferred_element_type=F32)
    xbuf[t, 0:LIVE, :] = packed.astype(BF16)

    def x_part(f, c):
        return xbuf.at[f, pl.ds(*CHUNKS[c]), :]

    def x_to(kind, f, c, device):
        remote(x_part(f, c), x_part(f, c), x_send.at[kind, c], x_recv.at[kind, c], device)

    def x_from(kind, f, c):
        arrived(x_part(f, c), x_recv.at[kind, c], x_send.at[kind, c])

    for c in range(4):
        x_to(0, t, c, y_next)
        x_to(1, t, c, y_prev)
        x_to(2, t, c, x_mate)

    spans = ((KEEP, 80 - KEEP), (0, KEEP), (0, KEEP), (KEEP, 80 - KEEP))

    def w_part(side, way, s, part, core_):
        first, count = spans[part]
        z_ = (z + (s if way else Z - s)) % Z
        return wbuf.at[pl.ds(pl.multiple_of(side * 2560 + z_ * 160 + core_ * 80 + first, 16), count), :]

    def w_rows(way, s, part, core_):
        return w_part(1 - xl if part > 1 else xl, way, s, part, core_)

    def last_way(part):
        return 1 if part == 2 else 0

    def z_hop(way, s, part):
        rows = w_rows(way, s, part, core)
        remote(rows, rows, z_send.at[way, s, part], z_recv.at[way, s, part], down if way else up)

    def to_mate(way, s, part):
        rows = w_rows(way, s, part, core)
        remote(rows, rows, c_send.at[way, s, part], c_recv.at[way, s, part], mate)

    def z_step(s):
        for part in range(3):
            for way in range(2):
                if s == 8 and last_way(part) != way:
                    continue
                rows = w_rows(way, s, part, core)
                arrived(rows, z_recv.at[way, s - 1, part], z_send.at[way, s - 1, part])
                if s < 7 or (s == 7 and last_way(part) == way):
                    z_hop(way, s, part)
                if part == 0:
                    remote(rows, rows, g_send.at[way, s], g_recv.at[way, s], across)
                to_mate(way, s, part)

    def x_step(s):
        for way in range(2):
            if s == 8 and way:
                continue
            arrived(w_rows(way, s, 3, core), g_recv.at[way, s], g_send.at[way, s])
            to_mate(way, s, 3)

    def from_mate(s):
        for part in range(4):
            for way in range(2):
                if (s == 8 and last_way(part) != way) or (s == 0 and way):
                    continue
                arrived(w_rows(way, s, part, 1 - core), c_recv.at[way, s, part], c_send.at[way, s, part])

    def start_ring():
        local[T].wait()
        for dx in range(2):
            for d in range(T):
                if dx or d:
                    slot = ((xl + dx) % 2) * T + (t + T - d) % T
                    arrived(piece.at[slot], piece_recv.at[dx, d], piece_send.at[dx, d])
        for half in range(2):
            side = 1 - xl if half else xl
            block = jnp.concatenate([piece[side * T + f].astype(F32) for f in range(T)], axis=0)
            wbuf[pl.ds(pl.multiple_of(side * 2560 + z * 160 + core * 80, 16), 80), :] = block.astype(BF16)
            for part in range(2 * half, 2 + half):
                for way in range(2):
                    z_hop(way, 0, part)
        for part in range(4):
            to_mate(0, 0, part)

    start_ring()

    sums = jnp.sum(packed * packed, axis=1, keepdims=True)
    sums = jnp.concatenate([jnp.broadcast_to(sums, (LIVE, 128)), jnp.zeros((640 - LIVE, 128), F32)], axis=0)
    dense = jnp.concatenate(
        [jnp.transpose(sums[128 * i : 128 * (i + 1)])[0:1] for i in range(5)] + [jnp.zeros((3, 128), F32)], axis=0
    )
    squares[t] = dense
    for d in range(1, T):
        remote(squares.at[t], squares.at[t], sq_send.at[d], sq_recv.at[d], tensor_peer(d))
    for f in range(T):
        gain = gain_ref[f * FEAT : (f + 1) * FEAT].astype(F32).reshape(1, FEAT)
        gains[f] = jnp.broadcast_to(gain, (8, FEAT))

    def norms():
        for copy in local[:T]:
            copy.wait()
        step_sum = jnp.zeros((STEPS, 1), F32)
        for f in range(T):
            part = xbuf[f, LIVE:ROWS, :].astype(F32)
            step_sum = step_sum + jnp.sum(part * part, axis=1, keepdims=True)
        for d in range(1, T):
            slot = squares.at[(t + T - d) % T]
            arrived(slot, sq_recv.at[d], sq_send.at[d])
        total_sq = squares[0]
        for f in range(1, T):
            total_sq = total_sq + squares[f]
        inv = lax.rsqrt(total_sq * (1.0 / MODEL_WIDTH) + 1e-6)
        for i in range(5):
            inverse[128 * i : 128 * (i + 1), :] = jnp.transpose(jnp.broadcast_to(inv[i : i + 1, :], (128, 128)))
        inverse[LIVE:ROWS, :] = jnp.broadcast_to(lax.rsqrt(step_sum * (1.0 / MODEL_WIDTH) + 1e-6), (STEPS, 128))

    def multiply(*blocks, first=False):
        parts = []
        for f in blocks:
            for i in range(5):
                lanes = slice(128 * i, 128 * (i + 1))
                part = xbuf[f, :, lanes].astype(F32) * inverse[0:ROWS, :]
                parts.append((part * gains[f, 0:1, lanes]).astype(BF16))
        weights = [wbuf[pl.ds(pl.multiple_of(f * FEAT, 128), FEAT), :] for f in blocks]
        product = jnp.dot(
            jnp.concatenate(parts, axis=1), jnp.concatenate(weights, axis=0), preferred_element_type=F32
        )
        acc[...] = product if first else acc[...] + product

    projected[ROWS:640, :] = jnp.zeros((640 - ROWS, COLS), BF16)
    slots, begin = [], jnp.int32(0)
    for j in range(DONE):
        earlier = jnp.int32(0)
        for i in range(j):
            earlier = earlier + jnp.where(target_ref[0, i] == target_ref[0, j], 1, 0)
        slots.append(target_ref[0, j] * CAP + earlier)
    for s in range(T * CAP):
        first_row, held = jnp.int32(0), jnp.int32(0)
        for j in range(DONE):
            hit = slots[j] == s
            first_row = first_row + jnp.where(hit, ends[j] - lens_ref[0, j], 0)
            held = held + jnp.where(hit, lens_ref[0, j], 0)
        starts[s] = first_row
        counts[s] = held

    def f_next(side, d=1):
        return side + (b + d) % 4

    own = a * 4

    def own_direct(c):
        x_from(0, f_next(own, 3), c)
        if c < 2:
            x_to(3, f_next(own, 3), c, y_next)
        x_from(1, f_next(own, 1), c)
        if c >= 2:
            x_to(4, f_next(own, 1), c, y_prev)

    def mate_direct(c):
        x_from(2, other + b, c)
        x_to(5, other + b, c, y_next)
        x_to(6, other + b, c, y_prev)

    def mate_relayed(c):
        x_from(5, f_next(other, 3), c)
        if c < 2:
            x_to(7, f_next(other, 3), c, y_next)
        x_from(6, f_next(other, 1), c)
        if c >= 2:
            x_to(8, f_next(other, 1), c, y_prev)

    def far(kind, side):
        for c in range(4):
            x_from(kind if c < 2 else kind + 1, f_next(side, 2), c)

    q, p = z // 4, z % 4
    near = (q + 3 + 2 * (p // 2)) % 4
    opposite = (q + 2) % 4
    wide_side = (q + 1 + 2 * (p // 2)) % 4

    def early(f):
        return ((f + 2 - b + 4) % 4 + 3) // 4

    keep = early(q)
    first_other, left = near + (q - near) * keep, q + (near - q) * keep
    keep = early(left)
    second_other, third_other = wide_side + (left - wide_side) * keep, left + (wide_side - left) * keep

    own_direct(0)
    mate_direct(0)
    z_step(1)
    own_direct(1)
    mate_direct(1)
    z_step(2)
    own_direct(2)
    mate_direct(2)
    x_step(1)
    z_step(3)
    own_direct(3)
    mate_direct(3)
    x_step(2)
    z_step(4)
    x_step(3)
    norms()
    z_step(5)
    mate_relayed(0)
    x_step(4)
    far(3, own)
    for s in range(4):
        from_mate(s)
    multiply(own + q, first=True)
    z_step(6)
    mate_relayed(1)
    mate_relayed(2)
    x_step(5)
    from_mate(4)
    z_step(7)
    mate_relayed(3)
    x_step(6)
    from_mate(5)
    multiply(own + near, other + first_other)
    z_step(8)
    x_step(7)
    from_mate(6)
    from_mate(7)
    x_step(8)
    multiply(own + wide_side, other + second_other)
    from_mate(8)
    multiply(own + opposite)
    far(7, other)
    multiply(other + third_other, other + opposite)

    scale = 1.0 / math.sqrt(HEAD_DIM)
    projected[0:ROWS, :] = (acc[...] + bias_ref[...].astype(F32).reshape(1, COLS)).astype(BF16)
    at_row = lax.broadcasted_iota(jnp.int32, (128, 128), 0)
    at_col = lax.broadcasted_iota(jnp.int32, (128, 128), 1)
    causal = (at_col <= at_row) & (at_col // LIMIT == at_row // LIMIT)

    def learner(dx, dy):
        return (a + dx) % 2 * 4 + (b + dy) % 4

    def spread(targets):
        picks = []
        for k in targets:
            first_row = jnp.where(at_row < LIMIT, starts[CAP * k], starts[CAP * k + 1] - LIMIT)
            wanted = first_row + at_row
            picks.append(
                jnp.concatenate(
                    [jnp.where(at_col + 128 * i == wanted, 1.0, 0.0).astype(BF16) for i in range(5)], axis=1
                )
            )
        picked = jnp.dot(jnp.concatenate(picks, axis=0), projected[...], preferred_element_type=F32)
        return [picked[128 * i : 128 * (i + 1)].astype(BF16) for i in range(len(targets))]

    def pair(k, rows):
        keys = rows[:, HEADS * HEAD_DIM : (HEADS + 1) * HEAD_DIM]
        vals = rows[:, (HEADS + 1) * HEAD_DIM :]
        held = jnp.where(at_row < LIMIT, counts[2 * k], counts[2 * k + 1] + LIMIT)
        live = at_row < held
        for g in range(HEADS):
            cols = slice(g * HEAD_DIM, (g + 1) * HEAD_DIM)
            scores = lax.dot_general(rows[:, cols], keys, NT, preferred_element_type=F32) * scale
            scores = jnp.where(causal, scores, -jnp.inf)
            powers = jnp.exp(scores - jnp.max(scores, axis=-1, keepdims=True))
            probs = (powers / jnp.sum(powers, axis=-1, keepdims=True)).astype(BF16)
            mixed = jnp.dot(probs, vals, preferred_element_type=F32)
            mixed = jnp.where(live, mixed, 0.0).astype(BF16)
            for h in range(CAP):
                attn[CAP * k + h, :, cols] = mixed[h * LIMIT : (h + 1) * LIMIT]

    def outgoing(k):
        return attn.at[pl.ds(CAP * k, CAP), :, :]

    def landing(f):
        return learn_out.at[:, :, pl.ds(pl.multiple_of(f * OUT, 128), OUT)]

    order = ((1, 2), (0, 2), (1, 1), (0, 1), (1, 3), (1, 0), (0, 3))
    targets = [learner(*step) for step in order] + [t]
    for n, k in enumerate(targets):
        if n % GROUP == 0:
            spreads = spread(targets[n : n + GROUP])
        pair(k, spreads[n % GROUP])
        if n < len(order):
            remote(outgoing(k), landing(t), a_send.at[n], a_recv.at[n], (r, k))
        else:
            bring(outgoing(t), landing(t))

    step_rows = projected[LIVE:ROWS, :]
    k_new = step_rows[:, HEADS * HEAD_DIM : (HEADS + 1) * HEAD_DIM].astype(F32)
    v_new = step_rows[:, (HEADS + 1) * HEAD_DIM :].astype(F32)
    qdec[...] = jnp.zeros_like(qdec)
    for g in range(HEADS):
        query = step_rows[:, g * HEAD_DIM : (g + 1) * HEAD_DIM].astype(F32)
        qdec[:, g, :] = query
    odec[:, 0, :] = k_new
    odec[:, 1, :] = v_new
    local[T + 1].wait()
    local[T + 2].wait()
    seen = lax.broadcasted_iota(jnp.int32, (8, CACHE), 1)

    def request(i, carry):
        query = qdec[i]
        fresh = odec[i]
        own_score = jnp.sum(query * fresh[0:1, :], axis=-1, keepdims=True) * scale
        scores = lax.dot_general(query.astype(BF16), kbuf[i], NT, preferred_element_type=F32) * scale
        filled = seen < stored_ref[0, i]
        peak = jnp.maximum(jnp.max(jnp.where(filled, scores, -jnp.inf), axis=-1, keepdims=True), own_score)
        powers = jnp.where(filled, jnp.exp(scores - peak), 0.0)
        own_power = jnp.exp(own_score - peak)
        whole = jnp.sum(powers, axis=-1, keepdims=True) + own_power
        probs = (powers / whole).astype(BF16)
        own_prob = (own_power / whole).astype(BF16).astype(F32)
        mixed = jnp.dot(probs, vbuf[i], preferred_element_type=F32)
        odec[i] = mixed + own_prob * fresh[1:2, :]
        return carry

    lax.fori_loop(0, STEPS, request, 0, unroll=4)
    for g in range(HEADS):
        dec_out[:, g * HEAD_DIM : (g + 1) * HEAD_DIM] = odec[:, g, :].astype(BF16)

    local[-1].wait()
    for n, (dx, dy) in enumerate(order):
        arrived(landing(learner(dx, 4 - dy)), a_recv.at[n], a_send.at[n])
    for copy in sent:
        copy.wait_send()


def hand_over(step_in, learner_in, step_out, learner_out, step_buf, buf, sem):
    def learner_part(ref, i):
        return ref.at[i // 4, (i % 4) * 16 : (i % 4 + 1) * 16, :]

    n = CAP * 4
    copies = [pltpu.make_async_copy(learner_part(learner_in, i), buf.at[i], sem.at[i]) for i in range(n)]
    copies.append(pltpu.make_async_copy(step_in, step_buf, sem.at[n]))
    outs = [pltpu.make_async_copy(buf.at[i], learner_part(learner_out, i), sem.at[n + 1 + i]) for i in range(n)]
    outs.append(pltpu.make_async_copy(step_buf, step_out, sem.at[2 * n + 1]))
    for copy in copies:
        copy.start()
    for copy, out in zip(copies, outs):
        copy.wait()
        out.start()
    for out in outs:
        out.wait()


def body(
    qkv_weight,
    qkv_bias,
    norm_gain,
    decode_hidden,
    stored_keys,
    stored_values,
    stored_lengths,
    response_hidden,
    response_lengths,
    response_target,
):
    vmem = pl.BlockSpec(memory_space=pltpu.VMEM)
    smem = pl.BlockSpec(memory_space=pltpu.SMEM)
    anywhere = pl.BlockSpec(memory_space=pl.ANY)
    dma = pltpu.SemaphoreType.DMA
    step, learner = pl.pallas_call(
        kernel,
        out_shape=(
            jax.ShapeDtypeStruct((STEPS, OUT), BF16),
            jax.ShapeDtypeStruct((CAP, LIMIT, T * OUT), BF16),
        ),
        in_specs=[smem, smem, smem, vmem, vmem, vmem, anywhere, vmem, anywhere, anywhere],
        out_specs=(vmem, anywhere),
        scratch_shapes=[
            pltpu.VMEM((2 * T, 10, COLS), BF16),
            pltpu.VMEM((MODEL_WIDTH, COLS), BF16),
            pltpu.VMEM((T, ROWS, FEAT), BF16),
            pltpu.VMEM((T, 8, 128), F32),
            pltpu.VMEM((640, 128), F32),
            pltpu.VMEM((T, 8, FEAT), F32),
            pltpu.VMEM((ROWS, COLS), F32),
            pltpu.VMEM((640, COLS), BF16),
            pltpu.VMEM((T * CAP, LIMIT, OUT), BF16),
            pltpu.VMEM((STEPS, CACHE, HEAD_DIM), BF16),
            pltpu.VMEM((STEPS, CACHE, HEAD_DIM), BF16),
            pltpu.VMEM((STEPS, 8, HEAD_DIM), F32),
            pltpu.VMEM((STEPS, 8, HEAD_DIM), F32),
            pltpu.SMEM((T * CAP,), jnp.int32),
            pltpu.SMEM((T * CAP,), jnp.int32),
            dma((2, T)), dma((2, T)),
            dma((T,)), dma((T,)),
            dma((9, 4)), dma((9, 4)),
            dma((2, 8, 3)), dma((2, 8, 3)),
            dma((2, 9, 4)), dma((2, 9, 4)),
            dma((2, 9)), dma((2, 9)),
            dma((T,)), dma((T,)),
            dma((T + 4,)),
        ],
        compiler_params=pltpu.CompilerParams(
            collective_id=0, has_side_effects=True, vmem_limit_bytes=56 << 20
        ),
        name="project_and_attend",
    )(
        response_lengths,
        response_target.reshape(1, DONE),
        stored_lengths,
        qkv_weight,
        qkv_bias,
        norm_gain,
        decode_hidden,
        response_hidden.reshape(DONE * LIMIT, FEAT),
        stored_keys.reshape(STEPS, CACHE, HEAD_DIM),
        stored_values.reshape(STEPS, CACHE, HEAD_DIM),
    )
    return pl.pallas_call(
        hand_over,
        out_shape=(
            jax.ShapeDtypeStruct(step.shape, BF16),
            jax.ShapeDtypeStruct(learner.shape, BF16),
        ),
        in_specs=[anywhere, anywhere],
        out_specs=(anywhere, anywhere),
        scratch_shapes=[
            pltpu.VMEM(step.shape, BF16),
            pltpu.VMEM((CAP * 4, 16, T * OUT), BF16),
            dma((2 + CAP * 8,)),
        ],
        name="hand_over",
    )(step, learner)


def solution(mesh):
    return jax.shard_map(
        body,
        mesh=mesh,
        in_specs=(
            P(("replica", "tensor"), None),
            P("tensor"),
            P(),
            P("replica", None),
            P("replica", "tensor", None, None),
            P("replica", "tensor", None, None),
            P("replica", None),
            P("replica", None, "tensor"),
            P("replica", None),
            P("replica", None),
        ),
        out_specs=(P("replica", "tensor"), P(("replica", "tensor"), None, None)),
        check_vma=False,
    )
```
